256 devices in a mesh: rows: 64 (over x, z_hi, y), experts: 4 (over z_lo, core).
Axes of the slice: x: 4, y: 4, z: 8 (z_hi: 4, z_lo: 2; z = z_hi * 2 + z_lo), core: 2. Of those that a mesh axis runs over, the one named last changes fastest.
Arguments:
- weight: bfloat16 [4, 64, 2048, 512], P('experts', None, 'rows'), may hold values from -3 to 3
- momentum: bfloat16 [4, 64, 2048, 512], P('experts', None, 'rows'), may hold values from -6 to 6
- gradient: bfloat16 [4, 64, 2048, 512], P('experts', None, 'rows'), may hold values from -32 to 32
- assign: int32 [4, 64], P('experts'), may hold values from 0 to 63, each once within a row
Outputs:
- new_weight: bfloat16 [4, 64, 2048, 512], P('experts', None, 'rows')
- new_momentum: bfloat16 [4, 64, 2048, 512], P('experts', None, 'rows')
The draws below stay inside these ranges and needn't reach their ends.
Inputs may be any that keep to these rules, and one draw needn't show every extreme that they name: Each row of assign names every slot 0 to 63 exactly once; matrix i of group e keeps its momentum in slot assign[e, i].
All inputs are finite; a program needn't handle non-finite values.
Results may differ from the reference program's by a relative error of at most 0.0075.
Values may be sent and summed in bfloat16 or wider, within the bound.
No kernel may reach another device: no remote copies, remote signals or barrier semaphores. Data moves between devices by JAX's collectives and lax.ppermute only.
A program may use at most 64 MiB of HBM per device.

```python
import math
import jax
import jax.numpy as jnp
from jax import lax

ROWS = 2048
COLS = 512
ITERS = 5
MATS = 64
GROUPS = 4


def draw_gradient(key, part):
    fourth = jax.random.fold_in(jax.random.fold_in(key, 11), 3)
    shape = (GROUPS, MATS, ROWS, COLS)
    row_pos = jnp.arange(ROWS, dtype=jnp.float32) / max(ROWS - 1, 1)
    group_pos = jnp.arange(GROUPS, dtype=jnp.float32) / max(GROUPS - 1, 1)
    scale = (1.0 + 2.0 * row_pos)[None, None, :, None] * (1.0 + 0.75 * group_pos)[:, None, None, None]
    values = scale * jax.random.normal(fourth, shape, jnp.float32)
    return jnp.clip(values, -32.0, 32.0).astype(jnp.bfloat16)


def block_scale(stream_key, dims, cuts, low, largest):
    factor_of = 1.0
    for axis_at, shards_of in cuts:
        steps = jax.random.uniform(jax.random.fold_in(jax.random.fold_in(stream_key, 6), axis_at), (shards_of,), jnp.float32, low / len(cuts), largest / len(cuts))
        factor_of = factor_of * jnp.repeat(jnp.exp(steps), dims[axis_at] // shards_of).reshape((-1,) + (1,) * (len(dims) - 1 - axis_at))
    return factor_of


def gaussian(key, dims, scale, most, cuts=(), held_as=jnp.bfloat16):
    result = jax.random.normal(key, dims, jnp.float32) * scale
    if len(cuts) > 0:
        result = block_scale(key, dims, cuts, -0.22, 0.18) * result
    return jnp.clip(result, min=-most, max=most).astype(held_as)


def setup_inputs(seed: int = 0) -> dict:
    arg_keys = jax.random.split(jax.random.key(seed), 5)
    weight = gaussian(arg_keys[0], (GROUPS, MATS, ROWS, COLS), 0.5, 3.0, ((0, 4), (2, 64)))
    momentum = gaussian(arg_keys[1], (GROUPS, MATS, ROWS, COLS), 1.0, 6.0, ((0, 4), (2, 64)))
    gradient = draw_gradient(jax.random.fold_in(arg_keys[4], 71), 0)
    assign = jax.vmap(lambda own: jax.random.permutation(own, MATS))(jax.random.split(arg_keys[3], GROUPS)).reshape((GROUPS, MATS)).astype(jnp.int32)
    return dict(weight=weight, momentum=momentum, gradient=gradient, assign=assign)


linear_coef = 3.4445
cubic_coef = -4.775
quintic_coef = 2.0315
beta_decay = 0.95
learn_rate = 0.5
weight_decay = 0.1
norm_epsilon = 1e-07
clip_epsilon = 1e-06

def orthogonal(update):
    widened = update.astype(jnp.float32)
    iterate = (widened / (jnp.sqrt(jnp.sum(widened * widened)) + norm_epsilon)).astype(jnp.bfloat16)
    for sweep in range(ITERS):
        gram_matrix = jnp.dot(iterate.T, iterate, preferred_element_type=jnp.float32).astype(jnp.bfloat16)
        square = jnp.dot(gram_matrix, gram_matrix, preferred_element_type=jnp.float32)
        polynomial = (cubic_coef * gram_matrix.astype(jnp.float32) + quintic_coef * square).astype(jnp.bfloat16)
        iterate = (linear_coef * iterate.astype(jnp.float32) + jnp.dot(iterate, polynomial, preferred_element_type=jnp.float32)).astype(jnp.bfloat16)
    return iterate

def reference(weight, momentum, gradient, assign):
    grad_wide = gradient.astype(jnp.float32)
    sum_squares = jnp.sum(grad_wide * grad_wide)
    clip_limit = math.sqrt(float(GROUPS * MATS * ROWS * COLS))
    clip_factor = jnp.minimum(1.0, clip_limit / (jnp.sqrt(sum_squares) + clip_epsilon))
    inverse = jnp.argsort(assign, axis=1).astype(jnp.int32)
    grad_slot = jnp.take_along_axis(grad_wide, inverse[:, :, None, None], axis=1)
    state = beta_decay * momentum.astype(jnp.float32) + clip_factor * grad_slot
    update = (clip_factor * grad_slot + beta_decay * state).astype(jnp.bfloat16)
    flat = update.reshape(GROUPS * MATS, ROWS, COLS)
    ortho_slot = lax.map(orthogonal, flat).reshape(GROUPS, MATS, ROWS, COLS)
    ortho = jnp.take_along_axis(ortho_slot, assign.astype(jnp.int32)[:, :, None, None], axis=1)
    shape_scale = 0.2 * math.sqrt(max(ROWS, COLS))
    new_weight = weight.astype(jnp.float32) * (1.0 - learn_rate * weight_decay) - learn_rate * shape_scale * ortho.astype(jnp.float32)
    return (new_weight.astype(jnp.bfloat16), state.astype(jnp.bfloat16))
```

```python
import functools
import math

import jax
import jax.numpy as jnp
from jax import lax
from jax.experimental import pallas as pl
from jax.experimental.pallas import tpu as pltpu
from jax.sharding import Mesh
from jax.sharding import PartitionSpec as P

ROWS = 2048
COLS = 512
ROWS_AXES = ("rows_0", "rows_1", "rows_2")
EXPERTS = ("experts_0", "experts_1")
ALL_AXES = ROWS_AXES + EXPERTS
DEVICES = 256
STAGES = (3, 2)

linear_coef = 3.4445
cubic_coef = -4.775
quintic_coef = 2.0315
beta_decay = 0.95
learn_rate = 0.5
weight_decay = 0.1
norm_epsilon = 1e-07
clip_epsilon = 1e-06
CHUNK = 8

bf16 = jnp.bfloat16
f32 = jnp.float32


def squares_kernel(grad_ref, out_ref, acc_ref):
    step = pl.program_id(0)

    @pl.when(step == 0)
    def _():
        acc_ref[...] = jnp.zeros_like(acc_ref)

    wide = grad_ref[...].astype(f32)
    acc_ref[...] += jnp.sum(wide * wide, axis=0)

    @pl.when(step == pl.num_programs(0) - 1)
    def _():
        folded = acc_ref[:, 0:128]
        for k in range(1, COLS // 128):
            folded = folded + acc_ref[:, 128 * k : 128 * (k + 1)]
        out_ref[...] = jnp.broadcast_to(jnp.sum(folded, axis=0, keepdims=True), out_ref.shape)


def partial_squares(grad):
    slots, rows, cols = grad.shape
    return pl.pallas_call(
        squares_kernel,
        grid=(slots // CHUNK,),
        in_specs=[pl.BlockSpec((CHUNK, rows, cols), lambda i: (i, 0, 0))],
        out_specs=pl.BlockSpec((DEVICES, 128), lambda i: (0, 0)),
        out_shape=jax.ShapeDtypeStruct((DEVICES, 128), f32),
        scratch_shapes=[pltpu.VMEM((rows, cols), f32)],
        compiler_params=pltpu.CompilerParams(vmem_limit_bytes=56 << 20),
        cost_estimate=pl.CostEstimate(flops=2 * grad.size, bytes_accessed=2 * grad.size, transcendentals=0),
        name="squares",
    )(grad)


def clip_from(partials, count):
    total = jnp.sum(partials)
    limit = math.sqrt(float(count))
    return jnp.minimum(1.0, limit / (jnp.sqrt(total) + clip_epsilon))


def fetch(chunk, slots_ref, grad_hbm, mom_hbm, grad_buf, mom_buf, sems):
    base = chunk * CHUNK
    pltpu.make_async_copy(
        grad_hbm.at[pl.ds(base, CHUNK)], grad_buf.at[pl.ds(base, CHUNK)], sems.at[0, chunk]
    ).start()
    for k in range(CHUNK):
        pltpu.make_async_copy(
            mom_hbm.at[slots_ref[base + k]], mom_buf.at[base + k], sems.at[1, chunk]
        ).start()


def await_fetch(chunk, grad_hbm, mom_hbm, grad_buf, mom_buf, sems):
    rows = pl.ds(chunk * CHUNK, CHUNK)
    pltpu.make_async_copy(grad_hbm.at[rows], grad_buf.at[rows], sems.at[0, chunk]).wait()
    pltpu.make_async_copy(mom_hbm.at[rows], mom_buf.at[rows], sems.at[1, chunk]).wait()


def update_kernel(count, slots_ref, part_ref, grad_hbm, mom_hbm, out_hbm, grad_buf, mom_buf, sems, out_sem):
    chunks = grad_buf.shape[0] // CHUNK
    for chunk in range(chunks):
        fetch(chunk, slots_ref, grad_hbm, mom_hbm, grad_buf, mom_buf, sems)
    clip = clip_from(part_ref[...], count)

    @pl.loop(0, chunks)
    def _(chunk):
        await_fetch(chunk, grad_hbm, mom_hbm, grad_buf, mom_buf, sems)
        rows = pl.ds(chunk * CHUNK, CHUNK)
        scaled = clip * grad_buf[rows].astype(f32)
        state = beta_decay * mom_buf[rows].astype(f32) + scaled
        mom_buf[rows] = (scaled + beta_decay * state).astype(bf16)
        pltpu.make_async_copy(mom_buf.at[rows], out_hbm.at[rows], out_sem.at[chunk]).start()

    for chunk in range(chunks):
        rows = pl.ds(chunk * CHUNK, CHUNK)
        pltpu.make_async_copy(mom_buf.at[rows], out_hbm.at[rows], out_sem.at[chunk]).wait()


def state_kernel(count, slots_ref, part_ref, grad_hbm, mom_hbm, out_hbm, grad_buf, mom_buf, sems, out_sem):
    chunks = grad_buf.shape[0] // CHUNK
    for chunk in range(chunks):
        fetch(chunk, slots_ref, grad_hbm, mom_hbm, grad_buf, mom_buf, sems)
    clip = clip_from(part_ref[...], count)

    @pl.loop(0, chunks)
    def _(chunk):
        await_fetch(chunk, grad_hbm, mom_hbm, grad_buf, mom_buf, sems)
        base = chunk * CHUNK
        rows = pl.ds(base, CHUNK)
        state = beta_decay * mom_buf[rows].astype(f32) + clip * grad_buf[rows].astype(f32)
        mom_buf[rows] = state.astype(bf16)
        for k in range(CHUNK):
            pltpu.make_async_copy(
                mom_buf.at[base + k], out_hbm.at[slots_ref[base + k]], out_sem.at[chunk]
            ).start()

    for chunk in range(chunks):
        rows = pl.ds(chunk * CHUNK, CHUNK)
        pltpu.make_async_copy(mom_buf.at[rows], out_hbm.at[rows], out_sem.at[chunk]).wait()


def momentum_call(kernel, name, count, slots, partials, grad, mom):
    chunks = grad.shape[0] // CHUNK
    return pl.pallas_call(
        functools.partial(kernel, count),
        grid_spec=pltpu.PrefetchScalarGridSpec(
            num_scalar_prefetch=1,
            grid=(1,),
            in_specs=[
                pl.BlockSpec(partials.shape, lambda i, s: (0, 0)),
                pl.BlockSpec(memory_space=pl.ANY),
                pl.BlockSpec(memory_space=pl.ANY),
            ],
            out_specs=pl.BlockSpec(memory_space=pl.ANY),
            scratch_shapes=[
                pltpu.VMEM(grad.shape, bf16),
                pltpu.VMEM(grad.shape, bf16),
                pltpu.SemaphoreType.DMA((2, chunks)),
                pltpu.SemaphoreType.DMA((chunks,)),
            ],
        ),
        out_shape=jax.ShapeDtypeStruct(grad.shape, bf16),
        compiler_params=pltpu.CompilerParams(vmem_limit_bytes=56 << 20),
        cost_estimate=pl.CostEstimate(flops=6 * grad.size, bytes_accessed=6 * grad.size, transcendentals=0),
        name=name,
    )(slots, partials, grad, mom)


def gram_of(tall_ref):
    tall = tall_ref[...]
    return lax.dot_general(tall, tall, (((0,), (0,)), ((), ())), preferred_element_type=f32)


def times(left, right):
    return jnp.dot(left, right, preferred_element_type=f32)


def composed(gram, steps):
    row = lax.broadcasted_iota(jnp.int32, gram.shape, 0)
    col = lax.broadcasted_iota(jnp.int32, gram.shape, 1)
    whole = None
    for step in range(steps):
        rounded = gram.astype(bf16)
        kept = rounded.astype(f32)
        poly = (cubic_coef * kept + quintic_coef * times(rounded, rounded)).astype(bf16)
        if whole is None:
            whole = poly.astype(f32) + jnp.where(row == col, linear_coef, 0.0)
        else:
            whole = linear_coef * whole + times(whole.astype(bf16), poly)
        if step + 1 < steps:
            half = linear_coef * kept + times(rounded, poly)
            gram = linear_coef * half + times(half.astype(bf16), poly)
    return whole.astype(bf16)


def orthogonal_kernel(in_ref, out_ref):
    gram = gram_of(in_ref)
    row = lax.broadcasted_iota(jnp.int32, gram.shape, 0)
    col = lax.broadcasted_iota(jnp.int32, gram.shape, 1)
    inverse = 1.0 / (jnp.sqrt(jnp.sum(jnp.where(row == col, gram, 0.0))) + norm_epsilon)
    factor = composed(gram * inverse * inverse, STAGES[0])
    tile = 256
    for k in range(ROWS // tile):
        rows = pl.ds(k * tile, tile)
        out_ref[rows] = (times(in_ref[rows], factor) * inverse).astype(bf16)
    for steps in STAGES[1:]:
        factor = composed(gram_of(out_ref), steps)
        for k in range(ROWS // tile):
            rows = pl.ds(k * tile, tile)
            out_ref[rows] = times(out_ref[rows], factor).astype(bf16)


def orthogonal(tall):
    return pl.pallas_call(
        orthogonal_kernel,
        out_shape=jax.ShapeDtypeStruct(tall.shape, bf16),
        compiler_params=pltpu.CompilerParams(
            vmem_limit_bytes=32 << 20
        ),
        cost_estimate=pl.CostEstimate(flops=8 * 10**9, bytes_accessed=4 * tall.size, transcendentals=0),
        name="orthogonal",
    )(tall)

def local(weight, momentum, gradient, assign):
    grad = gradient[0]
    mom = momentum[0]
    slots = assign[0]
    count = grad.size * lax.axis_size(ALL_AXES)
    shared = lax.all_to_all(
        partial_squares(grad).reshape(DEVICES, 1, 128), ALL_AXES, split_axis=0, concat_axis=0, tiled=True
    ).reshape(DEVICES, 128)
    update = momentum_call(update_kernel, "update", count, slots, shared, grad, mom)
    received = lax.all_to_all(update, ROWS_AXES, split_axis=0, concat_axis=0, tiled=True)
    state = momentum_call(state_kernel, "state", count, slots, shared, grad, mom)
    received, state = lax.optimization_barrier((received, state))
    result = orthogonal(received.reshape(ROWS, COLS)).reshape(received.shape)
    ortho = lax.all_to_all(result, ROWS_AXES, split_axis=0, concat_axis=0, tiled=True)
    shape_scale = 0.2 * math.sqrt(max(ROWS, COLS))
    new_weight = weight[0].astype(f32) * (1.0 - learn_rate * weight_decay) - (
        learn_rate * shape_scale
    ) * ortho.astype(f32)
    return (new_weight.astype(bf16)[None], state[None])


def solution(mesh):
    torus = Mesh(
        mesh.devices.reshape(4, 4, 4, 2, 2),
        ("rows_0", "rows_1", "rows_2", "experts_0", "experts_1"),
    )
    sharded = P(EXPERTS, None, ROWS_AXES, None)
    return jax.shard_map(
        local,
        mesh=torus,
        in_specs=(sharded, sharded, sharded, P(EXPERTS, None)),
        out_specs=(sharded, sharded),
        check_vma=False,
    )
```

```python
import functools
import math

import jax
import jax.numpy as jnp
from jax import lax
from jax.experimental import pallas as pl
from jax.experimental.pallas import tpu as pltpu
from jax.sharding import Mesh
from jax.sharding import PartitionSpec as P


ROWS = 2048
COLS = 512
ROWS_AXES = ("rows_0", "rows_1", "rows_2")
EXPERTS = ("experts_0", "experts_1")
ALL_AXES = ROWS_AXES + EXPERTS
DEVICES = 256
ITERS = 5
PLANE = ("rows_0", "rows_2")
DEPTH = "rows_1"
SENDING = ((2,), (1, 3), (0,))
RETURNING = ((0,), (1, 3), (2,))
SIDE = 128
BLOCKS = tuple((i, j) for i in range(4) for j in range(i, 4))

linear_coef = 3.4445
cubic_coef = -4.775
quintic_coef = 2.0315
beta_decay = 0.95
learn_rate = 0.5
weight_decay = 0.1
norm_epsilon = 1e-07
clip_epsilon = 1e-06
CHUNK = 8
LARGE_GRANT = 56 << 20
SMALL_GRANT = 16 << 20

bf16 = jnp.bfloat16
f32 = jnp.float32


def squares_kernel(grad_hbm, out_ref, grad_buf, acc_ref, sems):
    chunks = grad_buf.shape[0] // CHUNK
    for chunk in range(chunks):
        rows = pl.ds(chunk * CHUNK, CHUNK)
        pltpu.make_async_copy(grad_hbm.at[rows], grad_buf.at[rows], sems.at[chunk]).start()
    acc_ref[...] = jnp.zeros_like(acc_ref)

    @pl.loop(0, chunks)
    def _(chunk):
        rows = pl.ds(chunk * CHUNK, CHUNK)
        pltpu.make_async_copy(grad_hbm.at[rows], grad_buf.at[rows], sems.at[chunk]).wait()
        wide = grad_buf[rows].astype(f32)
        acc_ref[...] += jnp.sum(wide * wide, axis=0)

    folded = acc_ref[:, 0:128]
    for k in range(1, COLS // 128):
        folded = folded + acc_ref[:, 128 * k : 128 * (k + 1)]
    out_ref[...] = jnp.broadcast_to(jnp.sum(folded, axis=0, keepdims=True), out_ref.shape)


def partial_squares(grad):
    slots, rows, cols = grad.shape
    return pl.pallas_call(
        squares_kernel,
        in_specs=[pl.BlockSpec(memory_space=pltpu.HBM)],
        out_shape=jax.ShapeDtypeStruct((DEVICES, 128), f32),
        scratch_shapes=[
            pltpu.VMEM(grad.shape, bf16),
            pltpu.VMEM((rows, cols), f32),
            pltpu.SemaphoreType.DMA((slots // CHUNK,)),
        ],
        compiler_params=pltpu.CompilerParams(vmem_limit_bytes=LARGE_GRANT),
        cost_estimate=pl.CostEstimate(flops=2 * grad.size, bytes_accessed=2 * grad.size, transcendentals=0),
        name="squares",
    )(grad)


def clip_from(partials, count):
    total = jnp.sum(partials)
    limit = math.sqrt(float(count))
    return jnp.minimum(1.0, limit / (jnp.sqrt(total) + clip_epsilon))


def rows_of(peer, away, plane):
    return peer * 4 + lax.rem(plane + away, 4)


def pack_kernel(
    count, group, place_ref, slots_ref, part_ref, grad_hbm, mom_hbm, out_hbm, out_buf, grad_buf, mom_buf, sems, out_sem
):
    plane = place_ref[0]
    peers = out_buf.shape[0]
    rows = grad_buf.shape[2]
    for peer in range(peers):
        for k, away in enumerate(group):
            matrix = rows_of(peer, away, plane)
            pltpu.make_async_copy(grad_hbm.at[matrix], grad_buf.at[peer, k], sems.at[0, peer]).start()
            pltpu.make_async_copy(mom_hbm.at[slots_ref[matrix]], mom_buf.at[peer, k], sems.at[1, peer]).start()
    clip = clip_from(part_ref[...], count)

    @pl.loop(0, peers)
    def _(peer):
        pltpu.make_async_copy(grad_hbm.at[pl.ds(0, len(group))], grad_buf.at[peer], sems.at[0, peer]).wait()
        pltpu.make_async_copy(mom_hbm.at[pl.ds(0, len(group))], mom_buf.at[peer], sems.at[1, peer]).wait()
        for k in range(len(group)):
            scaled = clip * grad_buf[peer, k].astype(f32)
            state = beta_decay * mom_buf[peer, k].astype(f32) + scaled
            out_buf[peer, k * rows : (k + 1) * rows] = (scaled + beta_decay * state).astype(bf16)
        pltpu.make_async_copy(out_buf.at[peer], out_hbm.at[peer], out_sem).start()

    pltpu.make_async_copy(out_buf, out_hbm, out_sem).wait()


def packed(group, count, place, slots, partials, grad, mom):
    slot_count, rows, cols = grad.shape
    peers = slot_count // 4
    shape = (peers, len(group) * rows, cols)
    buffer = pltpu.VMEM((peers, len(group), rows, cols), bf16)
    size = peers * len(group) * rows * cols
    return pl.pallas_call(
        functools.partial(pack_kernel, count, group),
        grid_spec=pltpu.PrefetchScalarGridSpec(
            num_scalar_prefetch=2,
            grid=(1,),
            in_specs=[
                pl.BlockSpec(partials.shape, lambda i, p, s: (0, 0)),
                pl.BlockSpec(memory_space=pltpu.HBM),
                pl.BlockSpec(memory_space=pltpu.HBM),
            ],
            out_specs=pl.BlockSpec(memory_space=pltpu.HBM),
            scratch_shapes=[
                pltpu.VMEM(shape, bf16),
                buffer,
                buffer,
                pltpu.SemaphoreType.DMA((2, peers)),
                pltpu.SemaphoreType.DMA(()),
            ],
        ),
        out_shape=jax.ShapeDtypeStruct(shape, bf16),
        compiler_params=pltpu.CompilerParams(vmem_limit_bytes=LARGE_GRANT),
        cost_estimate=pl.CostEstimate(flops=6 * size, bytes_accessed=6 * size, transcendentals=0),
        name="pack",
    )(place, slots, partials, grad, mom)


def state_kernel(count, slots_ref, part_ref, grad_hbm, mom_hbm, out_hbm, grad_buf, mom_buf, sems, out_sem):
    chunks = grad_buf.shape[0] // CHUNK
    for chunk in range(chunks):
        base = chunk * CHUNK
        pltpu.make_async_copy(
            grad_hbm.at[pl.ds(base, CHUNK)], grad_buf.at[pl.ds(base, CHUNK)], sems.at[0, chunk]
        ).start()
        for k in range(CHUNK):
            pltpu.make_async_copy(
                mom_hbm.at[slots_ref[base + k]], mom_buf.at[base + k], sems.at[1, chunk]
            ).start()
    clip = clip_from(part_ref[...], count)

    @pl.loop(0, chunks)
    def _(chunk):
        base = chunk * CHUNK
        rows = pl.ds(base, CHUNK)
        pltpu.make_async_copy(grad_hbm.at[rows], grad_buf.at[rows], sems.at[0, chunk]).wait()
        pltpu.make_async_copy(mom_hbm.at[rows], mom_buf.at[rows], sems.at[1, chunk]).wait()
        state = beta_decay * mom_buf[rows].astype(f32) + clip * grad_buf[rows].astype(f32)
        mom_buf[rows] = state.astype(bf16)
        for k in range(CHUNK):
            pltpu.make_async_copy(
                mom_buf.at[base + k], out_hbm.at[slots_ref[base + k]], out_sem.at[chunk]
            ).start()

    for chunk in range(chunks):
        rows = pl.ds(chunk * CHUNK, CHUNK)
        pltpu.make_async_copy(mom_buf.at[rows], out_hbm.at[rows], out_sem.at[chunk]).wait()


def new_state(count, slots, partials, grad, mom):
    chunks = grad.shape[0] // CHUNK
    return pl.pallas_call(
        functools.partial(state_kernel, count),
        grid_spec=pltpu.PrefetchScalarGridSpec(
            num_scalar_prefetch=1,
            grid=(1,),
            in_specs=[
                pl.BlockSpec(partials.shape, lambda i, s: (0, 0)),
                pl.BlockSpec(memory_space=pltpu.HBM),
                pl.BlockSpec(memory_space=pltpu.HBM),
            ],
            out_specs=pl.BlockSpec(memory_space=pltpu.HBM),
            scratch_shapes=[
                pltpu.VMEM(grad.shape, bf16),
                pltpu.VMEM(grad.shape, bf16),
                pltpu.SemaphoreType.DMA((2, chunks)),
                pltpu.SemaphoreType.DMA((chunks,)),
            ],
        ),
        out_shape=jax.ShapeDtypeStruct(grad.shape, bf16),
        compiler_params=pltpu.CompilerParams(vmem_limit_bytes=LARGE_GRANT),
        cost_estimate=pl.CostEstimate(flops=6 * grad.size, bytes_accessed=6 * grad.size, transcendentals=0),
        name="state",
    )(slots, partials, grad, mom)


def times(left, right):
    return jnp.dot(left, right, preferred_element_type=f32)


def gram_of(tall):
    return lax.dot_general(tall, tall, (((0,), (0,)), ((), ())), preferred_element_type=f32)


def rows_at(in_ref, k):
    part = in_ref[:, k * (in_ref.shape[1] // 2) : (k + 1) * (in_ref.shape[1] // 2)] if k is not None else in_ref[...]
    return part.reshape(part.shape[0] * part.shape[1], part.shape[2])


def store_upper(out_ref, full):
    for n, (i, j) in enumerate(BLOCKS):
        out_ref[n * SIDE : (n + 1) * SIDE, :] = full[
            i * SIDE : (i + 1) * SIDE, j * SIDE : (j + 1) * SIDE
        ].astype(out_ref.dtype)


def load_full(full_ref, blocks):
    for n, (i, j) in enumerate(BLOCKS):
        block = blocks[n * SIDE : (n + 1) * SIDE, :]
        full_ref[i * SIDE : (i + 1) * SIDE, j * SIDE : (j + 1) * SIDE] = block.astype(full_ref.dtype)
        if i != j:
            full_ref[j * SIDE : (j + 1) * SIDE, i * SIDE : (i + 1) * SIDE] = block.T.astype(full_ref.dtype)


def gram_kernel(in_ref, *out_refs):
    for k, out_ref in enumerate(out_refs):
        store_upper(out_ref, gram_of(rows_at(in_ref, k if len(out_refs) > 1 else None)))


def partial_grams(received, group):
    shape = jax.ShapeDtypeStruct((len(BLOCKS) * SIDE, SIDE), bf16)
    return pl.pallas_call(
        gram_kernel,
        out_shape=[shape] * len(group),
        compiler_params=pltpu.CompilerParams(vmem_limit_bytes=SMALL_GRANT),
        cost_estimate=pl.CostEstimate(
            flops=2 * received.size * COLS, bytes_accessed=2 * received.size, transcendentals=0
        ),
        name="gram",
    )(received)


def composed(gram, steps):
    row = lax.broadcasted_iota(jnp.int32, gram.shape, 0)
    col = lax.broadcasted_iota(jnp.int32, gram.shape, 1)
    whole = None
    for step in range(steps):
        rounded = gram.astype(bf16)
        kept = rounded.astype(f32)
        poly = (cubic_coef * kept + quintic_coef * times(rounded, rounded)).astype(bf16)
        if whole is None:
            whole = poly.astype(f32) + jnp.where(row == col, linear_coef, 0.0)
        else:
            whole = linear_coef * whole + times(whole.astype(bf16), poly)
        if step + 1 < steps:
            half = linear_coef * kept + times(rounded, poly)
            gram = linear_coef * half + times(half.astype(bf16), poly)
    return whole


def factor_kernel(own_ref, a_ref, b_ref, c_ref, out_ref, full_ref):
    others = a_ref[...].astype(f32) + b_ref[...].astype(f32) + c_ref[...].astype(f32)
    load_full(full_ref, others)
    gram = gram_of(rows_at(own_ref, None)) + full_ref[...]
    row = lax.broadcasted_iota(jnp.int32, gram.shape, 0)
    col = lax.broadcasted_iota(jnp.int32, gram.shape, 1)
    inverse = 1.0 / (jnp.sqrt(jnp.sum(jnp.where(row == col, gram, 0.0))) + norm_epsilon)
    store_upper(out_ref, composed(gram * inverse * inverse, ITERS) * inverse)


def shared_factor(own, parts):
    return pl.pallas_call(
        factor_kernel,
        out_shape=jax.ShapeDtypeStruct((len(BLOCKS) * SIDE, SIDE), bf16),
        scratch_shapes=[pltpu.VMEM((COLS, COLS), f32)],
        compiler_params=pltpu.CompilerParams(vmem_limit_bytes=SMALL_GRANT),
        cost_estimate=pl.CostEstimate(flops=5 * 10**9, bytes_accessed=4 * own.size, transcendentals=0),
        name="factor",
    )(own, *parts)


def apply_kernel(in_ref, *refs):
    factors, (out_hbm, out_buf, full_ref, out_sem) = refs[:-4], refs[-4:]
    rows = in_ref.shape[1] // len(factors)
    for k, factor in enumerate(factors):
        load_full(full_ref, factor[...].astype(f32))
        product = times(rows_at(in_ref, k if len(factors) > 1 else None), full_ref[...])
        out_buf[:, k * rows : (k + 1) * rows] = product.reshape(in_ref.shape[0], rows, COLS).astype(bf16)
    copy = pltpu.make_async_copy(out_buf, out_hbm, out_sem)
    copy.start()
    copy.wait()


def applied(received, factors):
    return pl.pallas_call(
        apply_kernel,
        out_shape=jax.ShapeDtypeStruct(received.shape, bf16),
        out_specs=pl.BlockSpec(memory_space=pltpu.HBM),
        scratch_shapes=[
            pltpu.VMEM(received.shape, bf16),
            pltpu.VMEM((COLS, COLS), bf16),
            pltpu.SemaphoreType.DMA(()),
        ],
        compiler_params=pltpu.CompilerParams(vmem_limit_bytes=SMALL_GRANT),
        cost_estimate=pl.CostEstimate(
            flops=2 * received.size * COLS, bytes_accessed=4 * received.size, transcendentals=0
        ),
        name="apply",
    )(received, *factors)


def finish_kernel(group, place_ref, ortho_ref, weight_hbm, *refs):
    out_hbm, weight_buf, sems, out_sem = refs[-4:]
    plane = place_ref[0]
    peers = ortho_ref.shape[0]
    rows = weight_buf.shape[2]
    scale = learn_rate * 0.2 * math.sqrt(max(ROWS, COLS))
    for peer in range(peers):
        for k, away in enumerate(group):
            pltpu.make_async_copy(
                weight_hbm.at[rows_of(peer, away, plane)], weight_buf.at[peer, k], sems.at[peer]
            ).start()

    @pl.loop(0, peers)
    def _(peer):
        pltpu.make_async_copy(weight_hbm.at[pl.ds(0, len(group))], weight_buf.at[peer], sems.at[peer]).wait()
        for k, away in enumerate(group):
            ortho = ortho_ref[peer, k * rows : (k + 1) * rows].astype(f32)
            weight = weight_buf[peer, k].astype(f32)
            weight_buf[peer, k] = (weight * (1.0 - learn_rate * weight_decay) - scale * ortho).astype(bf16)
            pltpu.make_async_copy(
                weight_buf.at[peer, k], out_hbm.at[rows_of(peer, away, plane)], out_sem.at[peer]
            ).start()

    for peer in range(peers):
        pltpu.make_async_copy(weight_buf.at[peer], out_hbm.at[pl.ds(0, len(group))], out_sem.at[peer]).wait()


def finished(group, place, ortho, weight, before):
    peers = ortho.shape[0]
    rows = weight.shape[1]
    inplace = pl.BlockSpec(memory_space=pltpu.HBM)
    earlier = () if before is None else (before,)
    return pl.pallas_call(
        functools.partial(finish_kernel, group),
        grid_spec=pltpu.PrefetchScalarGridSpec(
            num_scalar_prefetch=1,
            grid=(1,),
            in_specs=[pl.BlockSpec(ortho.shape, lambda i, p: (0, 0, 0)), inplace] + [inplace] * len(earlier),
            out_specs=inplace,
            scratch_shapes=[
                pltpu.VMEM((peers, len(group), rows, COLS), bf16),
                pltpu.SemaphoreType.DMA((peers,)),
                pltpu.SemaphoreType.DMA((peers,)),
            ],
        ),
        out_shape=jax.ShapeDtypeStruct(weight.shape, bf16),
        input_output_aliases={3: 0} if earlier else {},
        compiler_params=pltpu.CompilerParams(vmem_limit_bytes=SMALL_GRANT),
        cost_estimate=pl.CostEstimate(flops=3 * ortho.size, bytes_accessed=6 * ortho.size, transcendentals=0),
        name="finish",
    )(place, ortho, weight, *earlier)


def shifted(value, planes):
    count = lax.axis_size(DEPTH)
    return lax.ppermute(value, DEPTH, [(k, (k + planes) % count) for k in range(count)])


def across(value):
    return lax.all_to_all(value, PLANE, split_axis=0, concat_axis=0, tiled=True)


def local(weight, momentum, gradient, assign):
    grad = gradient[0]
    mom = momentum[0]
    slots = assign[0]
    place = lax.axis_index(DEPTH).reshape(1)
    count = grad.size * lax.axis_size(ALL_AXES)
    shared = lax.all_to_all(
        partial_squares(grad).reshape(DEVICES, 1, 128), ALL_AXES, split_axis=0, concat_axis=0, tiled=True
    ).reshape(DEVICES, 128)
    held = {}
    parts = []
    for group in SENDING:
        ready = packed(group, count, place, slots, shared, grad, mom)
        held[group] = across(ready)
        if group == (0,):
            continue
        grams = partial_grams(held[group], group)
        for away, part in zip(group, grams):
            parts.append(shifted(part, away))
    state = new_state(count, slots, shared, grad, mom)
    factor = shared_factor(held[(0,)], parts)
    result = None
    for group in RETURNING:
        factors = []
        for away in group:
            factors.append(shifted(factor, -away) if away else factor)
        ready = applied(held[group], factors)
        ortho = across(ready)
        result = finished(group, place, ortho, weight[0], result)
    return (result[None], state[None])


def solution(mesh):
    torus = Mesh(
        mesh.devices.reshape(4, 4, 4, 2, 2),
        ("rows_0", "rows_1", "rows_2", "experts_0", "experts_1"),
    )
    sharded = P(EXPERTS, None, ROWS_AXES, None)
    return jax.shard_map(
        local,
        mesh=torus,
        in_specs=(sharded, sharded, sharded, P(EXPERTS, None)),
        out_specs=(sharded, sharded),
        check_vma=False,
    )
```

```python
import functools
import math

import jax
import jax.numpy as jnp
from jax import lax
from jax.experimental import pallas as pl
from jax.experimental.pallas import tpu as pltpu
from jax.sharding import Mesh
from jax.sharding import PartitionSpec as P


ROWS = 2048
COLS = 512
ROWS_AXES = ("rows_0", "rows_1", "rows_2")
EXPERTS = ("experts_0", "experts_1")
ALL_AXES = ROWS_AXES + EXPERTS
ITERS = 5
PLANE = ("rows_0", "rows_2")
DEPTH = "rows_1"
OTHERS = ("rows_1", "experts_0", "experts_1")
EARLY = 2
SENDING = ((1, 3), (0,))
RETURNING = ((0,), (1, 3), (2,))
SIDE = 128
BLOCKS = tuple((i, j) for i in range(4) for j in range(i, 4))

linear_coef = 3.4445
cubic_coef = -4.775
quintic_coef = 2.0315
beta_decay = 0.95
learn_rate = 0.5
weight_decay = 0.1
norm_epsilon = 1e-07
clip_epsilon = 1e-06
CHUNK = 8
LARGE_GRANT = 56 << 20
SMALL_GRANT = 16 << 20

bf16 = jnp.bfloat16
f32 = jnp.float32


def first_kernel(place_ref, slots_ref, grad_hbm, mom_hbm, out_hbm, grad_buf, acc_ref, out_buf, grad_sems, sems, out_sem):
    plane = place_ref[0]
    chunks = grad_buf.shape[0] // CHUNK
    peers, rows = out_buf.shape[0], grad_buf.shape[1]
    for chunk in range(chunks):
        part = pl.ds(chunk * CHUNK, CHUNK)
        pltpu.make_async_copy(grad_hbm.at[part], grad_buf.at[part], grad_sems.at[chunk]).start()
    for peer in range(peers):
        matrix = rows_of(peer, EARLY, plane)
        pltpu.make_async_copy(grad_hbm.at[matrix], out_buf.at[peer, pl.ds(0, rows)], sems.at[0]).start()
        pltpu.make_async_copy(
            mom_hbm.at[slots_ref[matrix]], out_buf.at[peer, pl.ds(rows, rows)], sems.at[1]
        ).start()
    acc_ref[...] = jnp.zeros_like(acc_ref)

    @pl.loop(0, chunks)
    def _(chunk):
        part = pl.ds(chunk * CHUNK, CHUNK)
        pltpu.make_async_copy(grad_hbm.at[part], grad_buf.at[part], grad_sems.at[chunk]).wait()
        wide = grad_buf[part].astype(f32)
        acc_ref[...] += jnp.sum(wide * wide, axis=0)

    folded = acc_ref[:, 0:128]
    for k in range(1, COLS // 128):
        folded = folded + acc_ref[:, 128 * k : 128 * (k + 1)]
    lanes = jnp.sum(folded, axis=0, keepdims=True)
    high = lanes.astype(bf16)
    rest = lanes - high.astype(f32)
    middle = rest.astype(bf16)
    low = (rest - middle.astype(f32)).astype(bf16)
    block = jnp.concatenate(
        [jnp.broadcast_to(term, (8, 128)) for term in (high, middle, low, jnp.zeros_like(low))], axis=1
    )
    for peer in range(peers):
        out_buf[peer, 2 * rows : 2 * rows + 8] = block
    blocks = grad_hbm.at[pl.ds(0, peers)]
    pltpu.make_async_copy(blocks, out_buf.at[:, pl.ds(0, rows)], sems.at[0]).wait()
    pltpu.make_async_copy(blocks, out_buf.at[:, pl.ds(rows, rows)], sems.at[1]).wait()
    copy = pltpu.make_async_copy(out_buf, out_hbm, out_sem)
    copy.start()
    copy.wait()


def first_chunk(place, slots, grad, mom):
    slot_count, rows, cols = grad.shape
    shape = (slot_count // 4, 2 * rows + 8, cols)
    return pl.pallas_call(
        first_kernel,
        grid_spec=pltpu.PrefetchScalarGridSpec(
            num_scalar_prefetch=2,
            grid=(1,),
            in_specs=[pl.BlockSpec(memory_space=pltpu.HBM)] * 2,
            out_specs=pl.BlockSpec(memory_space=pltpu.HBM),
            scratch_shapes=[
                pltpu.VMEM(grad.shape, bf16),
                pltpu.VMEM((rows, cols), f32),
                pltpu.VMEM(shape, bf16),
                pltpu.SemaphoreType.DMA((slot_count // CHUNK,)),
                pltpu.SemaphoreType.DMA((2,)),
                pltpu.SemaphoreType.DMA(()),
            ],
        ),
        out_shape=jax.ShapeDtypeStruct(shape, bf16),
        compiler_params=pltpu.CompilerParams(vmem_limit_bytes=LARGE_GRANT),
        cost_estimate=pl.CostEstimate(flops=2 * grad.size, bytes_accessed=5 * grad.size, transcendentals=0),
        name="first",
    )(place, slots, grad, mom)


def plane_kernel(in_ref, out_ref):
    total = jnp.zeros((8, 128), f32)
    start = in_ref.shape[1] - 8
    for peer in range(in_ref.shape[0]):
        for k in range(3):
            total = total + in_ref[peer, start:, 128 * k : 128 * (k + 1)].astype(f32)
    out_ref[...] = jnp.broadcast_to(total[None], out_ref.shape)


def plane_squares(received, others):
    return pl.pallas_call(
        plane_kernel,
        out_shape=jax.ShapeDtypeStruct((others, 8, 128), f32),
        compiler_params=pltpu.CompilerParams(vmem_limit_bytes=SMALL_GRANT),
        name="plane",
    )(received)


def clip_from(partials, count):
    total = jnp.sum(partials[:, 0, :])
    limit = math.sqrt(float(count))
    return jnp.minimum(1.0, limit / (jnp.sqrt(total) + clip_epsilon))


def rows_of(peer, away, plane):
    return peer * 4 + lax.rem(plane + away, 4)


def pack_kernel(
    count, group, place_ref, slots_ref, part_ref, grad_hbm, mom_hbm, out_hbm, out_buf, grad_buf, mom_buf, sems, out_sem
):
    plane = place_ref[0]
    peers = out_buf.shape[0]
    rows = grad_buf.shape[2]
    for peer in range(peers):
        for k, away in enumerate(group):
            matrix = rows_of(peer, away, plane)
            pltpu.make_async_copy(grad_hbm.at[matrix], grad_buf.at[peer, k], sems.at[0, peer]).start()
            pltpu.make_async_copy(mom_hbm.at[slots_ref[matrix]], mom_buf.at[peer, k], sems.at[1, peer]).start()
    clip = clip_from(part_ref[...], count)

    @pl.loop(0, peers)
    def _(peer):
        pltpu.make_async_copy(grad_hbm.at[pl.ds(0, len(group))], grad_buf.at[peer], sems.at[0, peer]).wait()
        pltpu.make_async_copy(mom_hbm.at[pl.ds(0, len(group))], mom_buf.at[peer], sems.at[1, peer]).wait()
        for k in range(len(group)):
            scaled = clip * grad_buf[peer, k].astype(f32)
            state = beta_decay * mom_buf[peer, k].astype(f32) + scaled
            out_buf[peer, k * rows : (k + 1) * rows] = (scaled + beta_decay * state).astype(bf16)
        pltpu.make_async_copy(out_buf.at[peer], out_hbm.at[peer], out_sem).start()

    pltpu.make_async_copy(out_buf, out_hbm, out_sem).wait()


def packed(group, count, place, slots, partials, grad, mom):
    slot_count, rows, cols = grad.shape
    peers = slot_count // 4
    shape = (peers, len(group) * rows, cols)
    buffer = pltpu.VMEM((peers, len(group), rows, cols), bf16)
    size = peers * len(group) * rows * cols
    return pl.pallas_call(
        functools.partial(pack_kernel, count, group),
        grid_spec=pltpu.PrefetchScalarGridSpec(
            num_scalar_prefetch=2,
            grid=(1,),
            in_specs=[
                pl.BlockSpec(partials.shape, lambda i, p, s: (0, 0, 0)),
                pl.BlockSpec(memory_space=pltpu.HBM),
                pl.BlockSpec(memory_space=pltpu.HBM),
            ],
            out_specs=pl.BlockSpec(memory_space=pltpu.HBM),
            scratch_shapes=[
                pltpu.VMEM(shape, bf16),
                buffer,
                buffer,
                pltpu.SemaphoreType.DMA((2, peers)),
                pltpu.SemaphoreType.DMA(()),
            ],
        ),
        out_shape=jax.ShapeDtypeStruct(shape, bf16),
        compiler_params=pltpu.CompilerParams(vmem_limit_bytes=LARGE_GRANT),
        cost_estimate=pl.CostEstimate(flops=6 * size, bytes_accessed=6 * size, transcendentals=0),
        name="pack",
    )(place, slots, partials, grad, mom)


def state_kernel(count, slots_ref, part_ref, grad_hbm, mom_hbm, out_hbm, grad_buf, mom_buf, sems, out_sem):
    chunks = grad_buf.shape[0] // CHUNK
    for chunk in range(chunks):
        base = chunk * CHUNK
        pltpu.make_async_copy(
            grad_hbm.at[pl.ds(base, CHUNK)], grad_buf.at[pl.ds(base, CHUNK)], sems.at[0, chunk]
        ).start()
        for k in range(CHUNK):
            pltpu.make_async_copy(
                mom_hbm.at[slots_ref[base + k]], mom_buf.at[base + k], sems.at[1, chunk]
            ).start()
    clip = clip_from(part_ref[...], count)

    @pl.loop(0, chunks)
    def _(chunk):
        base = chunk * CHUNK
        rows = pl.ds(base, CHUNK)
        pltpu.make_async_copy(grad_hbm.at[rows], grad_buf.at[rows], sems.at[0, chunk]).wait()
        pltpu.make_async_copy(mom_hbm.at[rows], mom_buf.at[rows], sems.at[1, chunk]).wait()
        state = beta_decay * mom_buf[rows].astype(f32) + clip * grad_buf[rows].astype(f32)
        mom_buf[rows] = state.astype(bf16)
        for k in range(CHUNK):
            pltpu.make_async_copy(
                mom_buf.at[base + k], out_hbm.at[slots_ref[base + k]], out_sem.at[chunk]
            ).start()

    for chunk in range(chunks):
        rows = pl.ds(chunk * CHUNK, CHUNK)
        pltpu.make_async_copy(mom_buf.at[rows], out_hbm.at[rows], out_sem.at[chunk]).wait()


def new_state(count, slots, partials, grad, mom):
    chunks = grad.shape[0] // CHUNK
    return pl.pallas_call(
        functools.partial(state_kernel, count),
        grid_spec=pltpu.PrefetchScalarGridSpec(
            num_scalar_prefetch=1,
            grid=(1,),
            in_specs=[
                pl.BlockSpec(partials.shape, lambda i, s: (0, 0, 0)),
                pl.BlockSpec(memory_space=pltpu.HBM),
                pl.BlockSpec(memory_space=pltpu.HBM),
            ],
            out_specs=pl.BlockSpec(memory_space=pltpu.HBM),
            scratch_shapes=[
                pltpu.VMEM(grad.shape, bf16),
                pltpu.VMEM(grad.shape, bf16),
                pltpu.SemaphoreType.DMA((2, chunks)),
                pltpu.SemaphoreType.DMA((chunks,)),
            ],
        ),
        out_shape=jax.ShapeDtypeStruct(grad.shape, bf16),
        compiler_params=pltpu.CompilerParams(vmem_limit_bytes=LARGE_GRANT),
        cost_estimate=pl.CostEstimate(flops=6 * grad.size, bytes_accessed=6 * grad.size, transcendentals=0),
        name="state",
    )(slots, partials, grad, mom)


def times(left, right):
    return jnp.dot(left, right, preferred_element_type=f32)


def gram_of(tall):
    return lax.dot_general(tall, tall, (((0,), (0,)), ((), ())), preferred_element_type=f32)


def rows_at(in_ref, k):
    part = in_ref[:, k * (in_ref.shape[1] // 2) : (k + 1) * (in_ref.shape[1] // 2)] if k is not None else in_ref[...]
    return part.reshape(part.shape[0] * part.shape[1], part.shape[2])


def store_upper(out_ref, full):
    for n, (i, j) in enumerate(BLOCKS):
        out_ref[n * SIDE : (n + 1) * SIDE, :] = full[
            i * SIDE : (i + 1) * SIDE, j * SIDE : (j + 1) * SIDE
        ].astype(out_ref.dtype)


def load_full(full_ref, blocks):
    for n, (i, j) in enumerate(BLOCKS):
        block = blocks[n * SIDE : (n + 1) * SIDE, :]
        full_ref[i * SIDE : (i + 1) * SIDE, j * SIDE : (j + 1) * SIDE] = block.astype(full_ref.dtype)
        if i != j:
            full_ref[j * SIDE : (j + 1) * SIDE, i * SIDE : (i + 1) * SIDE] = block.T.astype(full_ref.dtype)


def gram_kernel(in_ref, *out_refs):
    for k, out_ref in enumerate(out_refs):
        store_upper(out_ref, gram_of(rows_at(in_ref, k if len(out_refs) > 1 else None)))


def partial_grams(received, group):
    shape = jax.ShapeDtypeStruct((len(BLOCKS) * SIDE, SIDE), bf16)
    return pl.pallas_call(
        gram_kernel,
        out_shape=[shape] * len(group),
        compiler_params=pltpu.CompilerParams(vmem_limit_bytes=SMALL_GRANT),
        cost_estimate=pl.CostEstimate(
            flops=2 * received.size * COLS, bytes_accessed=2 * received.size, transcendentals=0
        ),
        name="gram",
    )(received)


def early_kernel(count, part_ref, in_ref, rows_ref, gram_ref):
    clip = clip_from(part_ref[...], count)
    rows = rows_ref.shape[1]
    scaled = clip * in_ref[:, 0:rows].astype(f32)
    state = beta_decay * in_ref[:, rows : 2 * rows].astype(f32) + scaled
    rows_ref[...] = (scaled + beta_decay * state).astype(bf16)
    store_upper(gram_ref, gram_of(rows_at(rows_ref, None)))


def early_gram(count, partials, received):
    peers, height, cols = received.shape
    return pl.pallas_call(
        functools.partial(early_kernel, count),
        out_shape=[
            jax.ShapeDtypeStruct((peers, (height - 8) // 2, cols), bf16),
            jax.ShapeDtypeStruct((len(BLOCKS) * SIDE, SIDE), bf16),
        ],
        compiler_params=pltpu.CompilerParams(vmem_limit_bytes=SMALL_GRANT),
        cost_estimate=pl.CostEstimate(
            flops=received.size * COLS, bytes_accessed=4 * received.size, transcendentals=0
        ),
        name="early",
    )(partials, received)


def composed(gram, steps):
    row = lax.broadcasted_iota(jnp.int32, gram.shape, 0)
    col = lax.broadcasted_iota(jnp.int32, gram.shape, 1)
    whole = None
    for step in range(steps):
        rounded = gram.astype(bf16)
        kept = rounded.astype(f32)
        poly = (cubic_coef * kept + quintic_coef * times(rounded, rounded)).astype(bf16)
        if whole is None:
            whole = poly.astype(f32) + jnp.where(row == col, linear_coef, 0.0)
        else:
            whole = linear_coef * whole + times(whole.astype(bf16), poly)
        if step + 1 < steps:
            half = linear_coef * kept + times(rounded, poly)
            gram = linear_coef * half + times(half.astype(bf16), poly)
    return whole


def factor_kernel(own_ref, a_ref, b_ref, c_ref, out_ref, full_ref):
    others = a_ref[...].astype(f32) + b_ref[...].astype(f32) + c_ref[...].astype(f32)
    load_full(full_ref, others)
    gram = gram_of(rows_at(own_ref, None)) + full_ref[...]
    row = lax.broadcasted_iota(jnp.int32, gram.shape, 0)
    col = lax.broadcasted_iota(jnp.int32, gram.shape, 1)
    inverse = 1.0 / (jnp.sqrt(jnp.sum(jnp.where(row == col, gram, 0.0))) + norm_epsilon)
    store_upper(out_ref, composed(gram * inverse * inverse, ITERS) * inverse)


def shared_factor(own, parts):
    return pl.pallas_call(
        factor_kernel,
        out_shape=jax.ShapeDtypeStruct((len(BLOCKS) * SIDE, SIDE), bf16),
        scratch_shapes=[pltpu.VMEM((COLS, COLS), f32)],
        compiler_params=pltpu.CompilerParams(vmem_limit_bytes=SMALL_GRANT),
        cost_estimate=pl.CostEstimate(flops=5 * 10**9, bytes_accessed=4 * own.size, transcendentals=0),
        name="factor",
    )(own, *parts)


def apply_kernel(in_ref, *refs):
    factors, (out_hbm, out_buf, full_ref, out_sem) = refs[:-4], refs[-4:]
    rows = in_ref.shape[1] // len(factors)
    for k, factor in enumerate(factors):
        load_full(full_ref, factor[...].astype(f32))
        product = times(rows_at(in_ref, k if len(factors) > 1 else None), full_ref[...])
        out_buf[:, k * rows : (k + 1) * rows] = product.reshape(in_ref.shape[0], rows, COLS).astype(bf16)
    copy = pltpu.make_async_copy(out_buf, out_hbm, out_sem)
    copy.start()
    copy.wait()


def applied(received, factors):
    return pl.pallas_call(
        apply_kernel,
        out_shape=jax.ShapeDtypeStruct(received.shape, bf16),
        out_specs=pl.BlockSpec(memory_space=pltpu.HBM),
        scratch_shapes=[
            pltpu.VMEM(received.shape, bf16),
            pltpu.VMEM((COLS, COLS), bf16),
            pltpu.SemaphoreType.DMA(()),
        ],
        compiler_params=pltpu.CompilerParams(vmem_limit_bytes=SMALL_GRANT),
        cost_estimate=pl.CostEstimate(
            flops=2 * received.size * COLS, bytes_accessed=4 * received.size, transcendentals=0
        ),
        name="apply",
    )(received, *factors)


def finish_kernel(group, place_ref, ortho_ref, weight_hbm, *refs):
    out_hbm, weight_buf, sems, out_sem = refs[-4:]
    plane = place_ref[0]
    peers = ortho_ref.shape[0]
    rows = weight_buf.shape[2]
    scale = learn_rate * 0.2 * math.sqrt(max(ROWS, COLS))
    for peer in range(peers):
        for k, away in enumerate(group):
            pltpu.make_async_copy(
                weight_hbm.at[rows_of(peer, away, plane)], weight_buf.at[peer, k], sems.at[peer]
            ).start()

    @pl.loop(0, peers)
    def _(peer):
        pltpu.make_async_copy(weight_hbm.at[pl.ds(0, len(group))], weight_buf.at[peer], sems.at[peer]).wait()
        for k, away in enumerate(group):
            ortho = ortho_ref[peer, k * rows : (k + 1) * rows].astype(f32)
            weight = weight_buf[peer, k].astype(f32)
            weight_buf[peer, k] = (weight * (1.0 - learn_rate * weight_decay) - scale * ortho).astype(bf16)
            pltpu.make_async_copy(
                weight_buf.at[peer, k], out_hbm.at[rows_of(peer, away, plane)], out_sem.at[peer]
            ).start()

    for peer in range(peers):
        pltpu.make_async_copy(weight_buf.at[peer], out_hbm.at[pl.ds(0, len(group))], out_sem.at[peer]).wait()


def finished(group, place, ortho, weight, before):
    peers = ortho.shape[0]
    rows = weight.shape[1]
    inplace = pl.BlockSpec(memory_space=pltpu.HBM)
    earlier = () if before is None else (before,)
    return pl.pallas_call(
        functools.partial(finish_kernel, group),
        grid_spec=pltpu.PrefetchScalarGridSpec(
            num_scalar_prefetch=1,
            grid=(1,),
            in_specs=[pl.BlockSpec(ortho.shape, lambda i, p: (0, 0, 0)), inplace] + [inplace] * len(earlier),
            out_specs=inplace,
            scratch_shapes=[
                pltpu.VMEM((peers, len(group), rows, COLS), bf16),
                pltpu.SemaphoreType.DMA((peers,)),
                pltpu.SemaphoreType.DMA((peers,)),
            ],
        ),
        out_shape=jax.ShapeDtypeStruct(weight.shape, bf16),
        input_output_aliases={3: 0} if earlier else {},
        compiler_params=pltpu.CompilerParams(vmem_limit_bytes=SMALL_GRANT),
        cost_estimate=pl.CostEstimate(flops=3 * ortho.size, bytes_accessed=6 * ortho.size, transcendentals=0),
        name="finish",
    )(place, ortho, weight, *earlier)


def shifted(value, planes):
    count = lax.axis_size(DEPTH)
    return lax.ppermute(value, DEPTH, [(k, (k + planes) % count) for k in range(count)])


def across(value):
    return lax.all_to_all(value, PLANE, split_axis=0, concat_axis=0, tiled=True)


def local(weight, momentum, gradient, assign):
    grad = gradient[0]
    mom = momentum[0]
    slots = assign[0]
    place = lax.axis_index(DEPTH).reshape(1)
    count = grad.size * lax.axis_size(ALL_AXES)
    held = {}
    parts = []
    early = across(first_chunk(place, slots, grad, mom))
    partial = plane_squares(early, lax.axis_size(OTHERS))
    shared = lax.all_to_all(partial, OTHERS, split_axis=0, concat_axis=0, tiled=True)
    held[(EARLY,)], part = early_gram(count, shared, early)
    parts.append(shifted(part, EARLY))
    for group in SENDING:
        ready = packed(group, count, place, slots, shared, grad, mom)
        held[group] = across(ready)
        if group == (0,):
            continue
        grams = partial_grams(held[group], group)
        for away, part in zip(group, grams):
            parts.append(shifted(part, away))
    state = new_state(count, slots, shared, grad, mom)
    factor = shared_factor(held[(0,)], parts)
    result = None
    for group in RETURNING:
        factors = []
        for away in group:
            factors.append(shifted(factor, -away) if away else factor)
        ready = applied(held[group], factors)
        ortho = across(ready)
        result = finished(group, place, ortho, weight[0], result)
    return (result[None], state[None])


def solution(mesh):
    torus = Mesh(
        mesh.devices.reshape(4, 4, 4, 2, 2),
        ("rows_0", "rows_1", "rows_2", "experts_0", "experts_1"),
    )
    sharded = P(EXPERTS, None, ROWS_AXES, None)
    return jax.shard_map(
        local,
        mesh=torus,
        in_specs=(sharded, sharded, sharded, P(EXPERTS, None)),
        out_specs=(sharded, sharded),
        check_vma=False,
    )
```

```python
import functools
import math

import jax
import jax.numpy as jnp
from jax import lax
from jax.experimental import pallas as pl
from jax.experimental.pallas import tpu as pltpu
from jax.sharding import Mesh
from jax.sharding import PartitionSpec as P

ROWS = 2048
COLS = 512
ROWS_AXES = ("rows_0", "rows_1", "rows_2")
EXPERTS = ("experts_0", "experts_1")
ALL_AXES = ROWS_AXES + EXPERTS
DEVICES = 256
STAGES = (3, 2)

linear_coef = 3.4445
cubic_coef = -4.775
quintic_coef = 2.0315
beta_decay = 0.95
learn_rate = 0.5
weight_decay = 0.1
norm_epsilon = 1e-07
clip_epsilon = 1e-06
CHUNK = 8
LARGE_GRANT = 56 << 20
SMALL_GRANT = 16 << 20
STAGE_GRANT = 48 << 20
UPDATE_GRANT = 16 << 20

bf16 = jnp.bfloat16
f32 = jnp.float32


def prepare_kernel(slots_ref, grad_hbm, mom_hbm, part_ref, grad_ref, mom_ref, acc_ref, grad_sems, sem):
    chunks = grad_ref.shape[0] // CHUNK
    for chunk in range(chunks):
        rows = pl.ds(chunk * CHUNK, CHUNK)
        pltpu.make_async_copy(grad_hbm.at[rows], grad_ref.at[rows], grad_sems.at[chunk]).start()
    for k in range(mom_ref.shape[0]):
        pltpu.make_async_copy(mom_hbm.at[slots_ref[k]], mom_ref.at[k], sem).start()
    acc_ref[...] = jnp.zeros_like(acc_ref)

    @pl.loop(0, chunks)
    def _(chunk):
        rows = pl.ds(chunk * CHUNK, CHUNK)
        pltpu.make_async_copy(grad_hbm.at[rows], grad_ref.at[rows], grad_sems.at[chunk]).wait()
        wide = grad_ref[rows].astype(f32)
        acc_ref[...] += jnp.sum(wide * wide, axis=0)

    folded = acc_ref[:, 0:128]
    for k in range(1, COLS // 128):
        folded = folded + acc_ref[:, 128 * k : 128 * (k + 1)]
    part_ref[...] = jnp.broadcast_to(jnp.sum(folded, axis=0, keepdims=True), part_ref.shape)
    pltpu.make_async_copy(mom_hbm, mom_ref, sem).wait()


def prepared(slots, grad, mom):
    whole = pl.BlockSpec(grad.shape, lambda i, s: (0, 0, 0))
    return pl.pallas_call(
        prepare_kernel,
        grid_spec=pltpu.PrefetchScalarGridSpec(
            num_scalar_prefetch=1,
            grid=(1,),
            in_specs=[pl.BlockSpec(memory_space=pl.ANY)] * 2,
            out_specs=[pl.BlockSpec((DEVICES, 128), lambda i, s: (0, 0)), whole, whole],
            scratch_shapes=[
                pltpu.VMEM(grad.shape[1:], f32),
                pltpu.SemaphoreType.DMA((grad.shape[0] // CHUNK,)),
                pltpu.SemaphoreType.DMA(()),
            ],
        ),
        out_shape=[
            jax.ShapeDtypeStruct((DEVICES, 128), f32),
            jax.ShapeDtypeStruct(grad.shape, bf16),
            jax.ShapeDtypeStruct(grad.shape, bf16),
        ],
        compiler_params=pltpu.CompilerParams(vmem_limit_bytes=STAGE_GRANT),
        cost_estimate=pl.CostEstimate(flops=2 * grad.size, bytes_accessed=8 * grad.size, transcendentals=0),
        name="prepare",
    )(slots, grad, mom)


def clip_from(partials, count):
    total = jnp.sum(partials)
    limit = math.sqrt(float(count))
    return jnp.minimum(1.0, limit / (jnp.sqrt(total) + clip_epsilon))


def fetch(chunk, slots_ref, grad_hbm, mom_hbm, grad_buf, mom_buf, sems):
    base = chunk * CHUNK
    pltpu.make_async_copy(
        grad_hbm.at[pl.ds(base, CHUNK)], grad_buf.at[pl.ds(base, CHUNK)], sems.at[0, chunk]
    ).start()
    for k in range(CHUNK):
        pltpu.make_async_copy(
            mom_hbm.at[slots_ref[base + k]], mom_buf.at[base + k], sems.at[1, chunk]
        ).start()


def await_fetch(chunk, grad_hbm, mom_hbm, grad_buf, mom_buf, sems):
    rows = pl.ds(chunk * CHUNK, CHUNK)
    pltpu.make_async_copy(grad_hbm.at[rows], grad_buf.at[rows], sems.at[0, chunk]).wait()
    pltpu.make_async_copy(mom_hbm.at[rows], mom_buf.at[rows], sems.at[1, chunk]).wait()


def update_kernel(count, part_ref, grad_ref, mom_ref, out_hbm, out_buf, sem):
    clip = clip_from(part_ref[...], count)

    @pl.loop(0, grad_ref.shape[0] // CHUNK)
    def _(chunk):
        rows = pl.ds(chunk * CHUNK, CHUNK)
        scaled = clip * grad_ref[rows].astype(f32)
        state = beta_decay * mom_ref[rows].astype(f32) + scaled
        out_buf[rows] = (scaled + beta_decay * state).astype(bf16)
        pltpu.make_async_copy(out_buf.at[rows], out_hbm.at[rows], sem).start()

    pltpu.make_async_copy(out_buf, out_hbm, sem).wait()


def updated(count, partials, grad, mom):
    return pl.pallas_call(
        functools.partial(update_kernel, count),
        out_specs=pl.BlockSpec(memory_space=pl.ANY),
        out_shape=jax.ShapeDtypeStruct(grad.shape, bf16),
        scratch_shapes=[pltpu.VMEM(grad.shape, bf16), pltpu.SemaphoreType.DMA(())],
        compiler_params=pltpu.CompilerParams(vmem_limit_bytes=UPDATE_GRANT),
        cost_estimate=pl.CostEstimate(flops=6 * grad.size, bytes_accessed=6 * grad.size, transcendentals=0),
        name="update",
    )(partials, grad, mom)


def state_kernel(count, slots_ref, part_ref, grad_hbm, mom_hbm, out_hbm, grad_buf, mom_buf, sems, out_sem):
    chunks = grad_buf.shape[0] // CHUNK
    for chunk in range(chunks):
        fetch(chunk, slots_ref, grad_hbm, mom_hbm, grad_buf, mom_buf, sems)
    clip = clip_from(part_ref[...], count)

    @pl.loop(0, chunks)
    def _(chunk):
        await_fetch(chunk, grad_hbm, mom_hbm, grad_buf, mom_buf, sems)
        base = chunk * CHUNK
        rows = pl.ds(base, CHUNK)
        state = beta_decay * mom_buf[rows].astype(f32) + clip * grad_buf[rows].astype(f32)
        mom_buf[rows] = state.astype(bf16)
        for k in range(CHUNK):
            pltpu.make_async_copy(
                mom_buf.at[base + k], out_hbm.at[slots_ref[base + k]], out_sem.at[chunk]
            ).start()

    for chunk in range(chunks):
        rows = pl.ds(chunk * CHUNK, CHUNK)
        pltpu.make_async_copy(mom_buf.at[rows], out_hbm.at[rows], out_sem.at[chunk]).wait()


def momentum_call(kernel, name, count, slots, partials, grad, mom):
    chunks = grad.shape[0] // CHUNK
    return pl.pallas_call(
        functools.partial(kernel, count),
        grid_spec=pltpu.PrefetchScalarGridSpec(
            num_scalar_prefetch=1,
            grid=(1,),
            in_specs=[
                pl.BlockSpec(partials.shape, lambda i, s: (0, 0)),
                pl.BlockSpec(memory_space=pl.ANY),
                pl.BlockSpec(memory_space=pl.ANY),
            ],
            out_specs=pl.BlockSpec(memory_space=pl.ANY),
            scratch_shapes=[
                pltpu.VMEM(grad.shape, bf16),
                pltpu.VMEM(grad.shape, bf16),
                pltpu.SemaphoreType.DMA((2, chunks)),
                pltpu.SemaphoreType.DMA((chunks,)),
            ],
        ),
        out_shape=jax.ShapeDtypeStruct(grad.shape, bf16),
        compiler_params=pltpu.CompilerParams(vmem_limit_bytes=LARGE_GRANT),
        cost_estimate=pl.CostEstimate(flops=6 * grad.size, bytes_accessed=6 * grad.size, transcendentals=0),
        name=name,
    )(slots, partials, grad, mom)


def gram_of(tall_ref):
    tall = tall_ref[...]
    return lax.dot_general(tall, tall, (((0,), (0,)), ((), ())), preferred_element_type=f32)


def times(left, right):
    return jnp.dot(left, right, preferred_element_type=f32)


def composed(gram, steps):
    row = lax.broadcasted_iota(jnp.int32, gram.shape, 0)
    col = lax.broadcasted_iota(jnp.int32, gram.shape, 1)
    whole = None
    for step in range(steps):
        rounded = gram.astype(bf16)
        kept = rounded.astype(f32)
        poly = (cubic_coef * kept + quintic_coef * times(rounded, rounded)).astype(bf16)
        if whole is None:
            whole = poly.astype(f32) + jnp.where(row == col, linear_coef, 0.0)
        else:
            whole = linear_coef * whole + times(whole.astype(bf16), poly)
        if step + 1 < steps:
            half = linear_coef * kept + times(rounded, poly)
            gram = linear_coef * half + times(half.astype(bf16), poly)
    return whole.astype(bf16)


def orthogonal_kernel(in_ref, out_ref):
    gram = gram_of(in_ref)
    row = lax.broadcasted_iota(jnp.int32, gram.shape, 0)
    col = lax.broadcasted_iota(jnp.int32, gram.shape, 1)
    inverse = 1.0 / (jnp.sqrt(jnp.sum(jnp.where(row == col, gram, 0.0))) + norm_epsilon)
    factor = composed(gram * inverse * inverse, STAGES[0])
    tile = 256
    for k in range(ROWS // tile):
        rows = pl.ds(k * tile, tile)
        out_ref[rows] = (times(in_ref[rows], factor) * inverse).astype(bf16)
    for steps in STAGES[1:]:
        factor = composed(gram_of(out_ref), steps)
        for k in range(ROWS // tile):
            rows = pl.ds(k * tile, tile)
            out_ref[rows] = times(out_ref[rows], factor).astype(bf16)


def orthogonal(tall):
    return pl.pallas_call(
        orthogonal_kernel,
        out_shape=jax.ShapeDtypeStruct(tall.shape, bf16),
        compiler_params=pltpu.CompilerParams(
            vmem_limit_bytes=32 << 20
        ),
        cost_estimate=pl.CostEstimate(flops=8 * 10**9, bytes_accessed=4 * tall.size, transcendentals=0),
        name="orthogonal",
    )(tall)

def finish_kernel(ortho_ref, weight_ref, out_hbm, out_buf, sem):
    scale = learn_rate * 0.2 * math.sqrt(max(ROWS, COLS))

    @pl.loop(0, ortho_ref.shape[0] // CHUNK)
    def _(chunk):
        rows = pl.ds(chunk * CHUNK, CHUNK)
        kept = weight_ref[rows].astype(f32) * (1.0 - learn_rate * weight_decay)
        out_buf[rows] = (kept - scale * ortho_ref[rows].astype(f32)).astype(bf16)
        pltpu.make_async_copy(out_buf.at[rows], out_hbm.at[rows], sem).start()

    pltpu.make_async_copy(out_buf, out_hbm, sem).wait()


def finished(ortho, weight):
    return pl.pallas_call(
        finish_kernel,
        out_specs=pl.BlockSpec(memory_space=pl.ANY),
        out_shape=jax.ShapeDtypeStruct(weight.shape, bf16),
        scratch_shapes=[pltpu.VMEM(weight.shape, bf16), pltpu.SemaphoreType.DMA(())],
        compiler_params=pltpu.CompilerParams(vmem_limit_bytes=SMALL_GRANT),
        cost_estimate=pl.CostEstimate(flops=3 * ortho.size, bytes_accessed=6 * ortho.size, transcendentals=0),
        name="finish",
    )(ortho, weight)


def local(weight, momentum, gradient, assign):
    grad = gradient[0]
    mom = momentum[0]
    slots = assign[0]
    count = grad.size * lax.axis_size(ALL_AXES)
    partials, near_grad, near_mom = prepared(slots, grad, mom)
    shared = lax.all_to_all(
        partials.reshape(DEVICES, 1, 128), ALL_AXES, split_axis=0, concat_axis=0, tiled=True
    ).reshape(DEVICES, 128)
    update = updated(count, shared, near_grad, near_mom)
    received = lax.all_to_all(update, ROWS_AXES, split_axis=0, concat_axis=0, tiled=True)
    state = momentum_call(state_kernel, "state", count, slots, shared, grad, mom)
    received, state = lax.optimization_barrier((received, state))
    result = orthogonal(received.reshape(ROWS, COLS)).reshape(received.shape)
    ortho = lax.all_to_all(result, ROWS_AXES, split_axis=0, concat_axis=0, tiled=True)
    return (finished(ortho, weight[0])[None], state[None])


def solution(mesh):
    torus = Mesh(
        mesh.devices.reshape(4, 4, 4, 2, 2),
        ("rows_0", "rows_1", "rows_2", "experts_0", "experts_1"),
    )
    sharded = P(EXPERTS, None, ROWS_AXES, None)
    return jax.shard_map(
        local,
        mesh=torus,
        in_specs=(sharded, sharded, sharded, P(EXPERTS, None)),
        out_specs=(sharded, sharded),
        check_vma=False,
    )
```

```python
import functools
import math

import jax
import jax.numpy as jnp
from jax import lax
from jax.experimental import pallas as pl
from jax.experimental.pallas import tpu as pltpu
from jax.sharding import Mesh
from jax.sharding import PartitionSpec as P


ROWS = 2048
COLS = 512
ROWS_AXES = ("rows_0", "rows_1", "rows_2")
EXPERTS = ("experts_0", "experts_1")
ALL_AXES = ROWS_AXES + EXPERTS
DEVICES = 256
ITERS = 5
DEPTH = "rows_1"
CORE = "experts_1"
SPREAD = ("rows_0", "rows_1", "rows_2", "experts_1")
SIDE = 128
BLOCKS = tuple((i, j) for i in range(4) for j in range(i, 4))

linear_coef = 3.4445
cubic_coef = -4.775
quintic_coef = 2.0315
beta_decay = 0.95
learn_rate = 0.5
weight_decay = 0.1
norm_epsilon = 1e-07
clip_epsilon = 1e-06
CHUNK = 8
LARGE_GRANT = 56 << 20
SMALL_GRANT = 16 << 20
STAGE_GRANT = 48 << 20
UPDATE_GRANT = 16 << 20

bf16 = jnp.bfloat16
f32 = jnp.float32


def exchange_groups():
    return [
        [
            ((x * 4 + (2 * pair + member + core) % 4) * 4 + y) * 2 + core
            for x in range(4)
            for member in range(2)
            for y in range(4)
        ]
        for core in range(2)
        for pair in range(2)
    ]


def rows_of(peer, away, pair):
    return peer * 2 + lax.rem(pair + away, 2)


def prepare_kernel(pair_ref, slots_ref, grad_hbm, mom_hbm, part_ref, grad_ref, mom_ref, acc_ref, grad_sems, sem):
    chunks = grad_ref.shape[0] // CHUNK
    half = grad_ref.shape[0] // 2
    pair = pair_ref[0]
    for k in range(2 * half):
        matrix = rows_of(k % half, 1 - k // half, pair)
        pltpu.make_async_copy(grad_hbm.at[matrix], grad_ref.at[k], grad_sems.at[k // CHUNK]).start()
    for k in range(2 * half):
        matrix = rows_of(k % half, 1 - k // half, pair)
        pltpu.make_async_copy(mom_hbm.at[slots_ref[matrix]], mom_ref.at[k], sem).start()
    acc_ref[...] = jnp.zeros_like(acc_ref)

    @pl.loop(0, chunks)
    def _(chunk):
        rows = pl.ds(chunk * CHUNK, CHUNK)
        pltpu.make_async_copy(grad_hbm.at[rows], grad_ref.at[rows], grad_sems.at[chunk]).wait()
        wide = grad_ref[rows].astype(f32)
        acc_ref[...] += jnp.sum(wide * wide, axis=0)

    folded = acc_ref[:, 0:128]
    for k in range(1, COLS // 128):
        folded = folded + acc_ref[:, 128 * k : 128 * (k + 1)]
    part_ref[...] = jnp.broadcast_to(jnp.sum(folded, axis=0, keepdims=True), part_ref.shape)
    pltpu.make_async_copy(mom_hbm, mom_ref, sem).wait()


def prepared(pair, slots, grad, mom):
    whole = pl.BlockSpec(grad.shape, lambda i, p, s: (0, 0, 0))
    return pl.pallas_call(
        prepare_kernel,
        grid_spec=pltpu.PrefetchScalarGridSpec(
            num_scalar_prefetch=2,
            grid=(1,),
            in_specs=[pl.BlockSpec(memory_space=pl.ANY)] * 2,
            out_specs=[pl.BlockSpec((DEVICES, 128), lambda i, p, s: (0, 0)), whole, whole],
            scratch_shapes=[
                pltpu.VMEM(grad.shape[1:], f32),
                pltpu.SemaphoreType.DMA((grad.shape[0] // CHUNK,)),
                pltpu.SemaphoreType.DMA(()),
            ],
        ),
        out_shape=[
            jax.ShapeDtypeStruct((DEVICES, 128), f32),
            jax.ShapeDtypeStruct(grad.shape, bf16),
            jax.ShapeDtypeStruct(grad.shape, bf16),
        ],
        compiler_params=pltpu.CompilerParams(vmem_limit_bytes=STAGE_GRANT),
        cost_estimate=pl.CostEstimate(flops=2 * grad.size, bytes_accessed=8 * grad.size, transcendentals=0),
        name="prepare",
    )(pair, slots, grad, mom)


def clip_from(partials, count):
    total = jnp.sum(partials)
    limit = math.sqrt(float(count))
    return jnp.minimum(1.0, limit / (jnp.sqrt(total) + clip_epsilon))


def fetch(chunk, slots_ref, grad_hbm, mom_hbm, grad_buf, mom_buf, sems):
    base = chunk * CHUNK
    pltpu.make_async_copy(
        grad_hbm.at[pl.ds(base, CHUNK)], grad_buf.at[pl.ds(base, CHUNK)], sems.at[0, chunk]
    ).start()
    for k in range(CHUNK):
        pltpu.make_async_copy(
            mom_hbm.at[slots_ref[base + k]], mom_buf.at[base + k], sems.at[1, chunk]
        ).start()


def await_fetch(chunk, grad_hbm, mom_hbm, grad_buf, mom_buf, sems):
    rows = pl.ds(chunk * CHUNK, CHUNK)
    pltpu.make_async_copy(grad_hbm.at[rows], grad_buf.at[rows], sems.at[0, chunk]).wait()
    pltpu.make_async_copy(mom_hbm.at[rows], mom_buf.at[rows], sems.at[1, chunk]).wait()


def update_kernel(count, first, part_ref, grad_ref, mom_ref, out_hbm, out_buf, sem):
    clip = clip_from(part_ref[...], count)

    @pl.loop(0, out_buf.shape[0] // CHUNK)
    def _(chunk):
        rows = pl.ds(chunk * CHUNK, CHUNK)
        source = pl.ds(first + chunk * CHUNK, CHUNK)
        scaled = clip * grad_ref[source].astype(f32)
        state = beta_decay * mom_ref[source].astype(f32) + scaled
        out_buf[rows] = (scaled + beta_decay * state).astype(bf16)
        pltpu.make_async_copy(out_buf.at[rows], out_hbm.at[rows], sem).start()

    pltpu.make_async_copy(out_buf, out_hbm, sem).wait()


def updated(count, away, partials, grad, mom):
    half = grad.shape[0] // 2
    shape = (half,) + grad.shape[1:]
    return pl.pallas_call(
        functools.partial(update_kernel, count, half * (1 - away)),
        out_specs=pl.BlockSpec(memory_space=pl.ANY),
        out_shape=jax.ShapeDtypeStruct(shape, bf16),
        scratch_shapes=[pltpu.VMEM(shape, bf16), pltpu.SemaphoreType.DMA(())],
        compiler_params=pltpu.CompilerParams(vmem_limit_bytes=UPDATE_GRANT),
        cost_estimate=pl.CostEstimate(flops=3 * grad.size, bytes_accessed=3 * grad.size, transcendentals=0),
        name="update",
    )(partials, grad, mom)


def state_kernel(count, slots_ref, part_ref, grad_hbm, mom_hbm, out_hbm, grad_buf, mom_buf, sems, out_sem):
    chunks = grad_buf.shape[0] // CHUNK
    for chunk in range(chunks):
        fetch(chunk, slots_ref, grad_hbm, mom_hbm, grad_buf, mom_buf, sems)
    clip = clip_from(part_ref[...], count)

    @pl.loop(0, chunks)
    def _(chunk):
        await_fetch(chunk, grad_hbm, mom_hbm, grad_buf, mom_buf, sems)
        base = chunk * CHUNK
        rows = pl.ds(base, CHUNK)
        state = beta_decay * mom_buf[rows].astype(f32) + clip * grad_buf[rows].astype(f32)
        mom_buf[rows] = state.astype(bf16)
        for k in range(CHUNK):
            pltpu.make_async_copy(
                mom_buf.at[base + k], out_hbm.at[slots_ref[base + k]], out_sem.at[chunk]
            ).start()

    for chunk in range(chunks):
        rows = pl.ds(chunk * CHUNK, CHUNK)
        pltpu.make_async_copy(mom_buf.at[rows], out_hbm.at[rows], out_sem.at[chunk]).wait()


def momentum_call(kernel, count, slots, partials, grad, mom):
    chunks = grad.shape[0] // CHUNK
    return pl.pallas_call(
        functools.partial(kernel, count),
        grid_spec=pltpu.PrefetchScalarGridSpec(
            num_scalar_prefetch=1,
            grid=(1,),
            in_specs=[
                pl.BlockSpec(partials.shape, lambda i, s: (0, 0)),
                pl.BlockSpec(memory_space=pl.ANY),
                pl.BlockSpec(memory_space=pl.ANY),
            ],
            out_specs=pl.BlockSpec(memory_space=pl.ANY),
            scratch_shapes=[
                pltpu.VMEM(grad.shape, bf16),
                pltpu.VMEM(grad.shape, bf16),
                pltpu.SemaphoreType.DMA((2, chunks)),
                pltpu.SemaphoreType.DMA((chunks,)),
            ],
        ),
        out_shape=jax.ShapeDtypeStruct(grad.shape, bf16),
        compiler_params=pltpu.CompilerParams(vmem_limit_bytes=LARGE_GRANT),
        cost_estimate=pl.CostEstimate(flops=6 * grad.size, bytes_accessed=6 * grad.size, transcendentals=0),
    )(slots, partials, grad, mom)


def times(left, right):
    return jnp.dot(left, right, preferred_element_type=f32)


def gram_of(tall):
    return lax.dot_general(tall, tall, (((0,), (0,)), ((), ())), preferred_element_type=f32)


def rows_at(in_ref):
    part = in_ref[...]
    return part.reshape(part.shape[0] * part.shape[1], part.shape[2])


def store_upper(out_ref, full):
    for n, (i, j) in enumerate(BLOCKS):
        out_ref[n * SIDE : (n + 1) * SIDE, :] = full[
            i * SIDE : (i + 1) * SIDE, j * SIDE : (j + 1) * SIDE
        ].astype(out_ref.dtype)


def load_full(full_ref, blocks):
    for n, (i, j) in enumerate(BLOCKS):
        block = blocks[n * SIDE : (n + 1) * SIDE, :]
        full_ref[i * SIDE : (i + 1) * SIDE, j * SIDE : (j + 1) * SIDE] = block.astype(full_ref.dtype)
        if i != j:
            full_ref[j * SIDE : (j + 1) * SIDE, i * SIDE : (i + 1) * SIDE] = block.T.astype(full_ref.dtype)


def gram_kernel(in_ref, out_ref):
    store_upper(out_ref, gram_of(rows_at(in_ref)))


def partial_gram(received):
    return pl.pallas_call(
        gram_kernel,
        out_shape=jax.ShapeDtypeStruct((len(BLOCKS) * SIDE, SIDE), bf16),
        compiler_params=pltpu.CompilerParams(vmem_limit_bytes=SMALL_GRANT),
        cost_estimate=pl.CostEstimate(
            flops=2 * received.size * COLS, bytes_accessed=2 * received.size, transcendentals=0
        ),
        name="gram",
    )(received)


def composed(gram, steps):
    row = lax.broadcasted_iota(jnp.int32, gram.shape, 0)
    col = lax.broadcasted_iota(jnp.int32, gram.shape, 1)
    whole = None
    for step in range(steps):
        rounded = gram.astype(bf16)
        kept = rounded.astype(f32)
        poly = (cubic_coef * kept + quintic_coef * times(rounded, rounded)).astype(bf16)
        if whole is None:
            whole = poly.astype(f32) + jnp.where(row == col, linear_coef, 0.0)
        else:
            whole = linear_coef * whole + times(whole.astype(bf16), poly)
        if step + 1 < steps:
            half = linear_coef * kept + times(rounded, poly)
            gram = linear_coef * half + times(half.astype(bf16), poly)
    return whole


def factor_kernel(own_ref, part_ref, out_ref, full_ref):
    load_full(full_ref, part_ref[...].astype(f32))
    gram = gram_of(rows_at(own_ref)) + full_ref[...]
    row = lax.broadcasted_iota(jnp.int32, gram.shape, 0)
    col = lax.broadcasted_iota(jnp.int32, gram.shape, 1)
    inverse = 1.0 / (jnp.sqrt(jnp.sum(jnp.where(row == col, gram, 0.0))) + norm_epsilon)
    store_upper(out_ref, composed(gram * inverse * inverse, ITERS) * inverse)


def shared_factor(own, part):
    return pl.pallas_call(
        factor_kernel,
        out_shape=jax.ShapeDtypeStruct((len(BLOCKS) * SIDE, SIDE), bf16),
        scratch_shapes=[pltpu.VMEM((COLS, COLS), f32)],
        compiler_params=pltpu.CompilerParams(vmem_limit_bytes=SMALL_GRANT),
        cost_estimate=pl.CostEstimate(flops=5 * 10**9, bytes_accessed=4 * own.size, transcendentals=0),
        name="factor",
    )(own, part)


def apply_kernel(in_ref, factor_ref, out_hbm, out_buf, full_ref, out_sem):
    load_full(full_ref, factor_ref[...].astype(f32))
    peers, rows, cols = in_ref.shape
    step = peers // 4

    for k in range(4):
        part = pl.ds(k * step, step)
        product = times(in_ref[part].reshape(step * rows, cols), full_ref[...])
        out_buf[part] = product.reshape(step, rows, cols).astype(bf16)
        pltpu.make_async_copy(out_buf.at[part], out_hbm.at[part], out_sem).start()
    pltpu.make_async_copy(out_buf, out_hbm, out_sem).wait()


def applied(received, factor):
    return pl.pallas_call(
        apply_kernel,
        out_specs=pl.BlockSpec(memory_space=pl.ANY),
        out_shape=jax.ShapeDtypeStruct(received.shape, bf16),
        scratch_shapes=[
            pltpu.VMEM(received.shape, bf16),
            pltpu.VMEM((COLS, COLS), bf16),
            pltpu.SemaphoreType.DMA(()),
        ],
        compiler_params=pltpu.CompilerParams(vmem_limit_bytes=SMALL_GRANT),
        cost_estimate=pl.CostEstimate(
            flops=2 * received.size * COLS, bytes_accessed=4 * received.size, transcendentals=0
        ),
        name="apply",
    )(received, factor)


def finish_kernel(group, place_ref, ortho_ref, weight_hbm, *refs):
    out_hbm, weight_buf, sems, out_sem = refs[-4:]
    plane = place_ref[0]
    peers = ortho_ref.shape[0]
    rows = weight_buf.shape[2]
    scale = learn_rate * 0.2 * math.sqrt(max(ROWS, COLS))
    for peer in range(peers):
        for k, away in enumerate(group):
            pltpu.make_async_copy(
                weight_hbm.at[rows_of(peer, away, plane)], weight_buf.at[peer, k], sems.at[peer]
            ).start()

    @pl.loop(0, peers)
    def _(peer):
        pltpu.make_async_copy(weight_hbm.at[pl.ds(0, len(group))], weight_buf.at[peer], sems.at[peer]).wait()
        for k, away in enumerate(group):
            ortho = ortho_ref[peer, k * rows : (k + 1) * rows].astype(f32)
            weight = weight_buf[peer, k].astype(f32)
            weight_buf[peer, k] = (weight * (1.0 - learn_rate * weight_decay) - scale * ortho).astype(bf16)
            pltpu.make_async_copy(
                weight_buf.at[peer, k], out_hbm.at[rows_of(peer, away, plane)], out_sem.at[peer]
            ).start()

    for peer in range(peers):
        pltpu.make_async_copy(weight_buf.at[peer], out_hbm.at[pl.ds(0, len(group))], out_sem.at[peer]).wait()


def finished(group, place, ortho, weight, before):
    peers = ortho.shape[0]
    rows = weight.shape[1]
    anywhere = pl.BlockSpec(memory_space=pl.ANY)
    earlier = () if before is None else (before,)
    return pl.pallas_call(
        functools.partial(finish_kernel, group),
        grid_spec=pltpu.PrefetchScalarGridSpec(
            num_scalar_prefetch=1,
            grid=(1,),
            in_specs=[pl.BlockSpec(ortho.shape, lambda i, p: (0, 0, 0)), anywhere] + [anywhere] * len(earlier),
            out_specs=anywhere,
            scratch_shapes=[
                pltpu.VMEM((peers, len(group), rows, COLS), bf16),
                pltpu.SemaphoreType.DMA((peers,)),
                pltpu.SemaphoreType.DMA((peers,)),
            ],
        ),
        out_shape=jax.ShapeDtypeStruct(weight.shape, bf16),
        input_output_aliases={3: 0} if earlier else {},
        compiler_params=pltpu.CompilerParams(vmem_limit_bytes=SMALL_GRANT),
        cost_estimate=pl.CostEstimate(flops=3 * ortho.size, bytes_accessed=6 * ortho.size, transcendentals=0),
        name="finish",
    )(place, ortho, weight, *earlier)


def across(value):
    return lax.all_to_all(
        value, SPREAD, split_axis=0, concat_axis=0, axis_index_groups=exchange_groups(), tiled=True
    )


def opposite(value):
    count = lax.axis_size(DEPTH)
    return lax.ppermute(value, DEPTH, [(k, (k + count // 2) % count) for k in range(count)])


def local(weight, momentum, gradient, assign):
    grad = gradient[0]
    mom = momentum[0]
    slots = assign[0]
    plane = lax.axis_index(DEPTH) + lax.axis_size(DEPTH) - lax.axis_index(CORE)
    pair = (lax.rem(plane, 4) // 2).reshape(1)
    count = grad.size * lax.axis_size(ALL_AXES)
    partials, near_grad, near_mom = prepared(pair, slots, grad, mom)
    shared = lax.all_to_all(
        partials.reshape(DEVICES, 1, 128), ALL_AXES, split_axis=0, concat_axis=0, tiled=True
    ).reshape(DEVICES, 128)
    ready = updated(count, 1, shared, near_grad, near_mom)
    far = across(ready)
    ready = updated(count, 0, shared, near_grad, near_mom)
    own = across(ready)
    part = partial_gram(far)
    part = opposite(part)
    state = momentum_call(state_kernel, count, slots, shared, grad, mom)
    factor = shared_factor(own, part)
    given = opposite(factor)
    ready = applied(own, factor)
    ortho = across(ready)
    result = finished((0,), pair, ortho, weight[0], None)
    ready = applied(far, given)
    ortho = across(ready)
    result = finished((1,), pair, ortho, weight[0], result)
    return (result[None], state[None])


def solution(mesh):
    torus = Mesh(
        mesh.devices.reshape(4, 4, 4, 2, 2),
        ("rows_0", "rows_1", "rows_2", "experts_0", "experts_1"),
    )
    sharded = P(EXPERTS, None, ROWS_AXES, None)
    return jax.shard_map(
        local,
        mesh=torus,
        in_specs=(sharded, sharded, sharded, P(EXPERTS, None)),
        out_specs=(sharded, sharded),
        check_vma=False,
    )
```

```python
import functools
import math

import jax
import jax.numpy as jnp
from jax import lax
from jax.experimental import pallas as pl
from jax.experimental.pallas import tpu as pltpu
from jax.sharding import Mesh
from jax.sharding import PartitionSpec as P

ROWS = 2048
COLS = 512
ROWS_AXES = ("rows_0", "rows_1", "rows_2")
EXPERTS = ("experts_0", "experts_1")
ALL_AXES = ROWS_AXES + EXPERTS
DEVICES = 256
ITERS = 5
DEPTH = "rows_1"
CORE = "experts_1"
SPREAD = ("rows_0", "rows_1", "rows_2", "experts_1")
SIDE = 128
BLOCKS = tuple((i, j) for i in range(4) for j in range(i, 4))

linear_coef = 3.4445
cubic_coef = -4.775
quintic_coef = 2.0315
beta_decay = 0.95
learn_rate = 0.5
weight_decay = 0.1
norm_epsilon = 1e-07
clip_epsilon = 1e-06
CHUNK = 8
LARGE_GRANT = 56 << 20
SMALL_GRANT = 16 << 20
STAGE_GRANT = 48 << 20
UPDATE_GRANT = 16 << 20

bf16 = jnp.bfloat16
f32 = jnp.float32


def exchange_groups():
    return [
        [
            ((x * 4 + (2 * pair + member + core) % 4) * 4 + y) * 2 + core
            for x in range(4)
            for member in range(2)
            for y in range(4)
        ]
        for core in range(2)
        for pair in range(2)
    ]


def rows_of(peer, away, pair):
    return peer * 2 + lax.rem(pair + away, 2)


def prepare_kernel(pair_ref, slots_ref, grad_hbm, mom_hbm, part_ref, grad_ref, mom_ref, acc_ref, grad_sems, sem):
    chunks = grad_ref.shape[0] // CHUNK
    pair = pair_ref[0]
    for k in range(grad_ref.shape[0]):
        matrix = rows_of(k // 2, 1 - k % 2, pair)
        pltpu.make_async_copy(grad_hbm.at[matrix], grad_ref.at[k], grad_sems.at[k // CHUNK]).start()
    for k in range(mom_ref.shape[0]):
        matrix = rows_of(k // 2, 1 - k % 2, pair)
        pltpu.make_async_copy(mom_hbm.at[slots_ref[matrix]], mom_ref.at[k], sem).start()
    acc_ref[...] = jnp.zeros_like(acc_ref)

    @pl.loop(0, chunks)
    def _(chunk):
        rows = pl.ds(chunk * CHUNK, CHUNK)
        pltpu.make_async_copy(grad_hbm.at[rows], grad_ref.at[rows], grad_sems.at[chunk]).wait()
        wide = grad_ref[rows].astype(f32)
        acc_ref[...] += jnp.sum(wide * wide, axis=0)

    folded = acc_ref[:, 0:128]
    for k in range(1, COLS // 128):
        folded = folded + acc_ref[:, 128 * k : 128 * (k + 1)]
    part_ref[...] = jnp.broadcast_to(jnp.sum(folded, axis=0, keepdims=True), part_ref.shape)
    pltpu.make_async_copy(mom_hbm, mom_ref, sem).wait()


def prepared(pair, slots, grad, mom):
    whole = pl.BlockSpec(grad.shape, lambda i, p, s: (0, 0, 0))
    return pl.pallas_call(
        prepare_kernel,
        grid_spec=pltpu.PrefetchScalarGridSpec(
            num_scalar_prefetch=2,
            grid=(1,),
            in_specs=[pl.BlockSpec(memory_space=pl.ANY)] * 2,
            out_specs=[pl.BlockSpec((DEVICES, 128), lambda i, p, s: (0, 0)), whole, whole],
            scratch_shapes=[
                pltpu.VMEM(grad.shape[1:], f32),
                pltpu.SemaphoreType.DMA((grad.shape[0] // CHUNK,)),
                pltpu.SemaphoreType.DMA(()),
            ],
        ),
        out_shape=[
            jax.ShapeDtypeStruct((DEVICES, 128), f32),
            jax.ShapeDtypeStruct(grad.shape, bf16),
            jax.ShapeDtypeStruct(grad.shape, bf16),
        ],
        compiler_params=pltpu.CompilerParams(vmem_limit_bytes=STAGE_GRANT),
        cost_estimate=pl.CostEstimate(flops=2 * grad.size, bytes_accessed=8 * grad.size, transcendentals=0),
        name="prepare",
    )(pair, slots, grad, mom)


def clip_from(partials, count):
    total = jnp.sum(partials)
    limit = math.sqrt(float(count))
    return jnp.minimum(1.0, limit / (jnp.sqrt(total) + clip_epsilon))


def fetch(chunk, slots_ref, grad_hbm, mom_hbm, grad_buf, mom_buf, sems):
    base = chunk * CHUNK
    pltpu.make_async_copy(
        grad_hbm.at[pl.ds(base, CHUNK)], grad_buf.at[pl.ds(base, CHUNK)], sems.at[0, chunk]
    ).start()
    for k in range(CHUNK):
        pltpu.make_async_copy(
            mom_hbm.at[slots_ref[base + k]], mom_buf.at[base + k], sems.at[1, chunk]
        ).start()


def await_fetch(chunk, grad_hbm, mom_hbm, grad_buf, mom_buf, sems):
    rows = pl.ds(chunk * CHUNK, CHUNK)
    pltpu.make_async_copy(grad_hbm.at[rows], grad_buf.at[rows], sems.at[0, chunk]).wait()
    pltpu.make_async_copy(mom_hbm.at[rows], mom_buf.at[rows], sems.at[1, chunk]).wait()


def update_kernel(count, part_ref, grad_ref, mom_ref, out_hbm, out_buf, sem):
    clip = clip_from(part_ref[...], count)

    @pl.loop(0, grad_ref.shape[0] // CHUNK)
    def _(chunk):
        rows = pl.ds(chunk * CHUNK, CHUNK)
        scaled = clip * grad_ref[rows].astype(f32)
        state = beta_decay * mom_ref[rows].astype(f32) + scaled
        out_buf[rows] = (scaled + beta_decay * state).astype(bf16)
        pltpu.make_async_copy(out_buf.at[rows], out_hbm.at[rows], sem).start()

    pltpu.make_async_copy(out_buf, out_hbm, sem).wait()


def updated(count, partials, grad, mom):
    return pl.pallas_call(
        functools.partial(update_kernel, count),
        out_specs=pl.BlockSpec(memory_space=pl.ANY),
        out_shape=jax.ShapeDtypeStruct(grad.shape, bf16),
        scratch_shapes=[pltpu.VMEM(grad.shape, bf16), pltpu.SemaphoreType.DMA(())],
        compiler_params=pltpu.CompilerParams(vmem_limit_bytes=UPDATE_GRANT),
        cost_estimate=pl.CostEstimate(flops=6 * grad.size, bytes_accessed=6 * grad.size, transcendentals=0),
        name="update",
    )(partials, grad, mom)


def state_kernel(count, slots_ref, part_ref, grad_hbm, mom_hbm, out_hbm, grad_buf, mom_buf, sems, out_sem):
    chunks = grad_buf.shape[0] // CHUNK
    for chunk in range(chunks):
        fetch(chunk, slots_ref, grad_hbm, mom_hbm, grad_buf, mom_buf, sems)
    clip = clip_from(part_ref[...], count)

    @pl.loop(0, chunks)
    def _(chunk):
        await_fetch(chunk, grad_hbm, mom_hbm, grad_buf, mom_buf, sems)
        base = chunk * CHUNK
        rows = pl.ds(base, CHUNK)
        state = beta_decay * mom_buf[rows].astype(f32) + clip * grad_buf[rows].astype(f32)
        mom_buf[rows] = state.astype(bf16)
        for k in range(CHUNK):
            pltpu.make_async_copy(
                mom_buf.at[base + k], out_hbm.at[slots_ref[base + k]], out_sem.at[chunk]
            ).start()

    for chunk in range(chunks):
        rows = pl.ds(chunk * CHUNK, CHUNK)
        pltpu.make_async_copy(mom_buf.at[rows], out_hbm.at[rows], out_sem.at[chunk]).wait()


def momentum_call(kernel, name, count, slots, partials, grad, mom):
    chunks = grad.shape[0] // CHUNK
    return pl.pallas_call(
        functools.partial(kernel, count),
        grid_spec=pltpu.PrefetchScalarGridSpec(
            num_scalar_prefetch=1,
            grid=(1,),
            in_specs=[
                pl.BlockSpec(partials.shape, lambda i, s: (0, 0)),
                pl.BlockSpec(memory_space=pl.ANY),
                pl.BlockSpec(memory_space=pl.ANY),
            ],
            out_specs=pl.BlockSpec(memory_space=pl.ANY),
            scratch_shapes=[
                pltpu.VMEM(grad.shape, bf16),
                pltpu.VMEM(grad.shape, bf16),
                pltpu.SemaphoreType.DMA((2, chunks)),
                pltpu.SemaphoreType.DMA((chunks,)),
            ],
        ),
        out_shape=jax.ShapeDtypeStruct(grad.shape, bf16),
        compiler_params=pltpu.CompilerParams(vmem_limit_bytes=LARGE_GRANT),
        cost_estimate=pl.CostEstimate(flops=6 * grad.size, bytes_accessed=6 * grad.size, transcendentals=0),
        name=name,
    )(slots, partials, grad, mom)


def times(left, right):
    return jnp.dot(left, right, preferred_element_type=f32)


def gram_of(tall):
    return lax.dot_general(tall, tall, (((0,), (0,)), ((), ())), preferred_element_type=f32)


def rows_at(in_ref, k):
    part = in_ref[:, k]
    return part.reshape(part.shape[0] * part.shape[1], part.shape[2])


def store_upper(out_ref, full):
    for n, (i, j) in enumerate(BLOCKS):
        out_ref[n * SIDE : (n + 1) * SIDE, :] = full[
            i * SIDE : (i + 1) * SIDE, j * SIDE : (j + 1) * SIDE
        ].astype(out_ref.dtype)


def load_full(full_ref, blocks):
    for n, (i, j) in enumerate(BLOCKS):
        block = blocks[n * SIDE : (n + 1) * SIDE, :]
        full_ref[i * SIDE : (i + 1) * SIDE, j * SIDE : (j + 1) * SIDE] = block.astype(full_ref.dtype)
        if i != j:
            full_ref[j * SIDE : (j + 1) * SIDE, i * SIDE : (i + 1) * SIDE] = block.T.astype(full_ref.dtype)


def far_kernel(in_ref, out_ref):
    store_upper(out_ref, gram_of(rows_at(in_ref, 0)))


def own_kernel(in_ref, out_ref):
    out_ref[...] = gram_of(rows_at(in_ref, 1))


def gram_call(kernel, name, received, shape):
    return pl.pallas_call(
        kernel,
        out_shape=shape,
        compiler_params=pltpu.CompilerParams(vmem_limit_bytes=SMALL_GRANT),
        cost_estimate=pl.CostEstimate(
            flops=received.size * COLS, bytes_accessed=2 * received.size, transcendentals=0
        ),
        name=name,
    )(received)


def composed(gram, steps):
    row = lax.broadcasted_iota(jnp.int32, gram.shape, 0)
    col = lax.broadcasted_iota(jnp.int32, gram.shape, 1)
    whole = None
    for step in range(steps):
        rounded = gram.astype(bf16)
        kept = rounded.astype(f32)
        poly = (cubic_coef * kept + quintic_coef * times(rounded, rounded)).astype(bf16)
        if whole is None:
            whole = poly.astype(f32) + jnp.where(row == col, linear_coef, 0.0)
        else:
            whole = linear_coef * whole + times(whole.astype(bf16), poly)
        if step + 1 < steps:
            half = linear_coef * kept + times(rounded, poly)
            gram = linear_coef * half + times(half.astype(bf16), poly)
    return whole


def factor_kernel(own_ref, part_ref, out_ref, full_ref):
    load_full(full_ref, part_ref[...].astype(f32))
    gram = own_ref[...] + full_ref[...]
    row = lax.broadcasted_iota(jnp.int32, gram.shape, 0)
    col = lax.broadcasted_iota(jnp.int32, gram.shape, 1)
    inverse = 1.0 / (jnp.sqrt(jnp.sum(jnp.where(row == col, gram, 0.0))) + norm_epsilon)
    store_upper(out_ref, composed(gram * inverse * inverse, ITERS) * inverse)


def shared_factor(own, part):
    return pl.pallas_call(
        factor_kernel,
        out_shape=jax.ShapeDtypeStruct((len(BLOCKS) * SIDE, SIDE), bf16),
        scratch_shapes=[pltpu.VMEM((COLS, COLS), f32)],
        compiler_params=pltpu.CompilerParams(vmem_limit_bytes=SMALL_GRANT),
        cost_estimate=pl.CostEstimate(flops=5 * 10**9, bytes_accessed=4 * own.size, transcendentals=0),
        name="factor",
    )(own, part)


def apply_kernel(which, in_ref, factor_ref, *refs):
    out_hbm, out_buf, full_ref, out_sem = refs[-4:]
    load_full(full_ref, factor_ref[...].astype(f32))
    peers, _, rows, cols = in_ref.shape
    step = peers // 4
    for k in range(4):
        part = pl.ds(k * step, step)
        product = times(in_ref[part, which].reshape(step * rows, cols), full_ref[...])
        out_buf[part] = product.reshape(step, rows, cols).astype(bf16)
        pltpu.make_async_copy(out_buf.at[part], out_hbm.at[part, which], out_sem).start()
    pltpu.make_async_copy(out_buf, out_hbm.at[:, which], out_sem).wait()


def applied(which, received, factor, before):
    earlier = () if before is None else (before,)
    vmem = pl.BlockSpec(memory_space=pltpu.VMEM)
    anywhere = pl.BlockSpec(memory_space=pl.ANY)
    return pl.pallas_call(
        functools.partial(apply_kernel, which),
        in_specs=[vmem, vmem] + [anywhere] * len(earlier),
        out_specs=anywhere,
        out_shape=jax.ShapeDtypeStruct(received.shape, bf16),
        scratch_shapes=[
            pltpu.VMEM(received.shape[:1] + received.shape[2:], bf16),
            pltpu.VMEM((COLS, COLS), bf16),
            pltpu.SemaphoreType.DMA(()),
        ],
        input_output_aliases={2: 0} if earlier else {},
        compiler_params=pltpu.CompilerParams(vmem_limit_bytes=SMALL_GRANT),
        cost_estimate=pl.CostEstimate(
            flops=received.size * COLS, bytes_accessed=3 * received.size, transcendentals=0
        ),
        name="apply",
    )(received, factor, *earlier)


def finish_kernel(pair_ref, ortho_ref, weight_ref, out_hbm, out_buf, sem):
    scale = learn_rate * 0.2 * math.sqrt(max(ROWS, COLS))
    pair = pair_ref[0]

    @pl.loop(0, ortho_ref.shape[0] // CHUNK)
    def _(chunk):
        base = chunk * CHUNK
        for k in range(CHUNK):
            matrix = base + rows_of(k // 2, 1 - k % 2, pair)
            kept = weight_ref[matrix].astype(f32) * (1.0 - learn_rate * weight_decay)
            out_buf[matrix] = (kept - scale * ortho_ref[base + k].astype(f32)).astype(bf16)
        rows = pl.ds(base, CHUNK)
        pltpu.make_async_copy(out_buf.at[rows], out_hbm.at[rows], sem).start()

    pltpu.make_async_copy(out_buf, out_hbm, sem).wait()


def finished(pair, ortho, weight):
    whole = pl.BlockSpec(weight.shape, lambda i, p: (0, 0, 0))
    return pl.pallas_call(
        finish_kernel,
        grid_spec=pltpu.PrefetchScalarGridSpec(
            num_scalar_prefetch=1,
            grid=(1,),
            in_specs=[whole, whole],
            out_specs=pl.BlockSpec(memory_space=pl.ANY),
            scratch_shapes=[pltpu.VMEM(weight.shape, bf16), pltpu.SemaphoreType.DMA(())],
        ),
        out_shape=jax.ShapeDtypeStruct(weight.shape, bf16),
        compiler_params=pltpu.CompilerParams(vmem_limit_bytes=24 << 20),
        cost_estimate=pl.CostEstimate(flops=3 * ortho.size, bytes_accessed=6 * ortho.size, transcendentals=0),
        name="finish",
    )(pair, ortho, weight)


def across(value):
    return lax.all_to_all(
        value, SPREAD, split_axis=0, concat_axis=0, axis_index_groups=exchange_groups(), tiled=True
    )


def opposite(value):
    count = lax.axis_size(DEPTH)
    return lax.ppermute(value, DEPTH, [(k, (k + count // 2) % count) for k in range(count)])


def local(weight, momentum, gradient, assign):
    grad = gradient[0]
    mom = momentum[0]
    slots = assign[0]
    plane = lax.axis_index(DEPTH) + lax.axis_size(DEPTH) - lax.axis_index(CORE)
    pair = (lax.rem(plane, 4) // 2).reshape(1)
    count = grad.size * lax.axis_size(ALL_AXES)
    partials, near_grad, near_mom = prepared(pair, slots, grad, mom)
    shared = lax.all_to_all(
        partials.reshape(DEVICES, 1, 128), ALL_AXES, split_axis=0, concat_axis=0, tiled=True
    ).reshape(DEVICES, 128)
    update = updated(count, shared, near_grad, near_mom)
    received = across(update)
    state = momentum_call(state_kernel, "state", count, slots, shared, grad, mom)
    received, state = lax.optimization_barrier((received, state))
    halves = received.reshape(-1, 2, *received.shape[1:])
    upper = jax.ShapeDtypeStruct((len(BLOCKS) * SIDE, SIDE), bf16)
    part = opposite(gram_call(far_kernel, "far", halves, upper))
    own = gram_call(own_kernel, "own", halves, jax.ShapeDtypeStruct((COLS, COLS), f32))
    factor = shared_factor(own, part)
    given = opposite(factor)
    result = applied(0, halves, given, applied(1, halves, factor, None))
    ortho = across(result.reshape(received.shape))
    return (finished(pair, ortho, weight[0])[None], state[None])


def solution(mesh):
    torus = Mesh(
        mesh.devices.reshape(4, 4, 4, 2, 2),
        ("rows_0", "rows_1", "rows_2", "experts_0", "experts_1"),
    )
    sharded = P(EXPERTS, None, ROWS_AXES, None)
    return jax.shard_map(
        local,
        mesh=torus,
        in_specs=(sharded, sharded, sharded, P(EXPERTS, None)),
        out_specs=(sharded, sharded),
        check_vma=False,
    )
```

```python
import functools
import math

import jax
import jax.numpy as jnp
from jax import lax
from jax.experimental import pallas as pl
from jax.experimental.pallas import tpu as pltpu
from jax.sharding import Mesh
from jax.sharding import PartitionSpec as P

ROWS = 2048
COLS = 512
ROWS_AXES = ("rows_0", "rows_1", "rows_2")
EXPERTS = ("experts_0", "experts_1")
ALL_AXES = ROWS_AXES + EXPERTS
DEVICES = 256
ITERS = 5
DEPTH = "rows_1"
CORE = "experts_1"
SPREAD = ("rows_0", "rows_1", "rows_2", "experts_1")
SIDE = 128
BLOCKS = tuple((i, j) for i in range(4) for j in range(i, 4))

linear_coef = 3.4445
cubic_coef = -4.775
quintic_coef = 2.0315
beta_decay = 0.95
learn_rate = 0.5
weight_decay = 0.1
norm_epsilon = 1e-07
clip_epsilon = 1e-06
CHUNK = 8
LARGE_GRANT = 56 << 20
SMALL_GRANT = 16 << 20
STAGE_GRANT = 48 << 20
UPDATE_GRANT = 16 << 20

bf16 = jnp.bfloat16
f32 = jnp.float32


def exchange_groups():
    return [
        [
            ((x * 4 + (2 * pair + member + core) % 4) * 4 + y) * 2 + core
            for x in range(4)
            for member in range(2)
            for y in range(4)
        ]
        for core in range(2)
        for pair in range(2)
    ]


def rows_of(peer, away, pair):
    return (peer ^ 4) * 2 + 1 - pair if away else peer * 2 + pair


def prepare_kernel(pair_ref, slots_ref, grad_hbm, mom_hbm, part_ref, grad_ref, mom_ref, acc_ref, grad_sems, sem):
    chunks = grad_ref.shape[0] // CHUNK
    pair = pair_ref[0]
    for k in range(grad_ref.shape[0]):
        matrix = rows_of(k // 2, 1 - k % 2, pair)
        pltpu.make_async_copy(grad_hbm.at[matrix], grad_ref.at[k], grad_sems.at[k // CHUNK]).start()
    for k in range(mom_ref.shape[0]):
        matrix = rows_of(k // 2, 1 - k % 2, pair)
        pltpu.make_async_copy(mom_hbm.at[slots_ref[matrix]], mom_ref.at[k], sem).start()
    acc_ref[...] = jnp.zeros_like(acc_ref)

    @pl.loop(0, chunks)
    def _(chunk):
        rows = pl.ds(chunk * CHUNK, CHUNK)
        pltpu.make_async_copy(grad_hbm.at[rows], grad_ref.at[rows], grad_sems.at[chunk]).wait()
        wide = grad_ref[rows].astype(f32)
        acc_ref[...] += jnp.sum(wide * wide, axis=0)

    folded = acc_ref[:, 0:128]
    for k in range(1, COLS // 128):
        folded = folded + acc_ref[:, 128 * k : 128 * (k + 1)]
    part_ref[...] = jnp.broadcast_to(jnp.sum(folded, axis=0, keepdims=True), part_ref.shape)
    pltpu.make_async_copy(mom_hbm, mom_ref, sem).wait()


def prepared(pair, slots, grad, mom):
    whole = pl.BlockSpec(grad.shape, lambda i, p, s: (0, 0, 0))
    return pl.pallas_call(
        prepare_kernel,
        grid_spec=pltpu.PrefetchScalarGridSpec(
            num_scalar_prefetch=2,
            grid=(1,),
            in_specs=[pl.BlockSpec(memory_space=pl.ANY)] * 2,
            out_specs=[pl.BlockSpec((DEVICES, 128), lambda i, p, s: (0, 0)), whole, whole],
            scratch_shapes=[
                pltpu.VMEM(grad.shape[1:], f32),
                pltpu.SemaphoreType.DMA((grad.shape[0] // CHUNK,)),
                pltpu.SemaphoreType.DMA(()),
            ],
        ),
        out_shape=[
            jax.ShapeDtypeStruct((DEVICES, 128), f32),
            jax.ShapeDtypeStruct(grad.shape, bf16),
            jax.ShapeDtypeStruct(grad.shape, bf16),
        ],
        compiler_params=pltpu.CompilerParams(vmem_limit_bytes=STAGE_GRANT),
        cost_estimate=pl.CostEstimate(flops=2 * grad.size, bytes_accessed=8 * grad.size, transcendentals=0),
        name="prepare",
    )(pair, slots, grad, mom)


def clip_from(partials, count):
    total = jnp.sum(partials)
    limit = math.sqrt(float(count))
    return jnp.minimum(1.0, limit / (jnp.sqrt(total) + clip_epsilon))


def fetch(chunk, slots_ref, grad_hbm, mom_hbm, grad_buf, mom_buf, sems):
    base = chunk * CHUNK
    pltpu.make_async_copy(
        grad_hbm.at[pl.ds(base, CHUNK)], grad_buf.at[pl.ds(base, CHUNK)], sems.at[0, chunk]
    ).start()
    for k in range(CHUNK):
        pltpu.make_async_copy(
            mom_hbm.at[slots_ref[base + k]], mom_buf.at[base + k], sems.at[1, chunk]
        ).start()


def await_fetch(chunk, grad_hbm, mom_hbm, grad_buf, mom_buf, sems):
    rows = pl.ds(chunk * CHUNK, CHUNK)
    pltpu.make_async_copy(grad_hbm.at[rows], grad_buf.at[rows], sems.at[0, chunk]).wait()
    pltpu.make_async_copy(mom_hbm.at[rows], mom_buf.at[rows], sems.at[1, chunk]).wait()


def update_kernel(count, part_ref, grad_ref, mom_ref, out_hbm, out_buf, sem):
    clip = clip_from(part_ref[...], count)

    @pl.loop(0, grad_ref.shape[0] // CHUNK)
    def _(chunk):
        rows = pl.ds(chunk * CHUNK, CHUNK)
        scaled = clip * grad_ref[rows].astype(f32)
        state = beta_decay * mom_ref[rows].astype(f32) + scaled
        out_buf[rows] = (scaled + beta_decay * state).astype(bf16)
        pltpu.make_async_copy(out_buf.at[rows], out_hbm.at[rows], sem).start()

    pltpu.make_async_copy(out_buf, out_hbm, sem).wait()


def updated(count, partials, grad, mom):
    return pl.pallas_call(
        functools.partial(update_kernel, count),
        out_specs=pl.BlockSpec(memory_space=pl.ANY),
        out_shape=jax.ShapeDtypeStruct(grad.shape, bf16),
        scratch_shapes=[pltpu.VMEM(grad.shape, bf16), pltpu.SemaphoreType.DMA(())],
        compiler_params=pltpu.CompilerParams(vmem_limit_bytes=UPDATE_GRANT),
        cost_estimate=pl.CostEstimate(flops=6 * grad.size, bytes_accessed=6 * grad.size, transcendentals=0),
        name="update",
    )(partials, grad, mom)


def state_kernel(count, slots_ref, part_ref, grad_hbm, mom_hbm, out_hbm, grad_buf, mom_buf, sems, out_sem):
    chunks = grad_buf.shape[0] // CHUNK
    for chunk in range(chunks):
        fetch(chunk, slots_ref, grad_hbm, mom_hbm, grad_buf, mom_buf, sems)
    clip = clip_from(part_ref[...], count)

    @pl.loop(0, chunks)
    def _(chunk):
        await_fetch(chunk, grad_hbm, mom_hbm, grad_buf, mom_buf, sems)
        base = chunk * CHUNK
        rows = pl.ds(base, CHUNK)
        state = beta_decay * mom_buf[rows].astype(f32) + clip * grad_buf[rows].astype(f32)
        mom_buf[rows] = state.astype(bf16)
        for k in range(CHUNK):
            pltpu.make_async_copy(
                mom_buf.at[base + k], out_hbm.at[slots_ref[base + k]], out_sem.at[chunk]
            ).start()

    for chunk in range(chunks):
        rows = pl.ds(chunk * CHUNK, CHUNK)
        pltpu.make_async_copy(mom_buf.at[rows], out_hbm.at[rows], out_sem.at[chunk]).wait()


def momentum_call(kernel, name, count, slots, partials, grad, mom):
    chunks = grad.shape[0] // CHUNK
    return pl.pallas_call(
        functools.partial(kernel, count),
        grid_spec=pltpu.PrefetchScalarGridSpec(
            num_scalar_prefetch=1,
            grid=(1,),
            in_specs=[
                pl.BlockSpec(partials.shape, lambda i, s: (0, 0)),
                pl.BlockSpec(memory_space=pl.ANY),
                pl.BlockSpec(memory_space=pl.ANY),
            ],
            out_specs=pl.BlockSpec(memory_space=pl.ANY),
            scratch_shapes=[
                pltpu.VMEM(grad.shape, bf16),
                pltpu.VMEM(grad.shape, bf16),
                pltpu.SemaphoreType.DMA((2, chunks)),
                pltpu.SemaphoreType.DMA((chunks,)),
            ],
        ),
        out_shape=jax.ShapeDtypeStruct(grad.shape, bf16),
        compiler_params=pltpu.CompilerParams(vmem_limit_bytes=LARGE_GRANT),
        cost_estimate=pl.CostEstimate(flops=6 * grad.size, bytes_accessed=6 * grad.size, transcendentals=0),
        name=name,
    )(slots, partials, grad, mom)


def times(left, right):
    return jnp.dot(left, right, preferred_element_type=f32)


def gram_of(tall):
    return lax.dot_general(tall, tall, (((0,), (0,)), ((), ())), preferred_element_type=f32)


def rows_at(in_ref, k):
    part = in_ref[:, k]
    return part.reshape(part.shape[0] * part.shape[1], part.shape[2])


def store_upper(out_ref, full):
    for n, (i, j) in enumerate(BLOCKS):
        out_ref[n * SIDE : (n + 1) * SIDE, :] = full[
            i * SIDE : (i + 1) * SIDE, j * SIDE : (j + 1) * SIDE
        ].astype(out_ref.dtype)


def load_full(full_ref, blocks):
    for n, (i, j) in enumerate(BLOCKS):
        block = blocks[n * SIDE : (n + 1) * SIDE, :]
        full_ref[i * SIDE : (i + 1) * SIDE, j * SIDE : (j + 1) * SIDE] = block.astype(full_ref.dtype)
        if i != j:
            full_ref[j * SIDE : (j + 1) * SIDE, i * SIDE : (i + 1) * SIDE] = block.T.astype(full_ref.dtype)


def far_kernel(in_ref, out_ref):
    store_upper(out_ref, gram_of(rows_at(in_ref, 0)))


def own_kernel(in_ref, out_ref):
    out_ref[...] = gram_of(rows_at(in_ref, 1))


def gram_call(kernel, name, received, shape):
    return pl.pallas_call(
        kernel,
        out_shape=shape,
        compiler_params=pltpu.CompilerParams(vmem_limit_bytes=SMALL_GRANT),
        cost_estimate=pl.CostEstimate(
            flops=received.size * COLS, bytes_accessed=2 * received.size, transcendentals=0
        ),
        name=name,
    )(received)


def composed(gram, steps):
    row = lax.broadcasted_iota(jnp.int32, gram.shape, 0)
    col = lax.broadcasted_iota(jnp.int32, gram.shape, 1)
    whole = None
    for step in range(steps):
        rounded = gram.astype(bf16)
        kept = rounded.astype(f32)
        poly = (cubic_coef * kept + quintic_coef * times(rounded, rounded)).astype(bf16)
        if whole is None:
            whole = poly.astype(f32) + jnp.where(row == col, linear_coef, 0.0)
        else:
            whole = linear_coef * whole + times(whole.astype(bf16), poly)
        if step + 1 < steps:
            half = linear_coef * kept + times(rounded, poly)
            gram = linear_coef * half + times(half.astype(bf16), poly)
    return whole


def factor_kernel(own_ref, part_ref, out_ref, full_ref):
    load_full(full_ref, part_ref[...].astype(f32))
    gram = own_ref[...] + full_ref[...]
    row = lax.broadcasted_iota(jnp.int32, gram.shape, 0)
    col = lax.broadcasted_iota(jnp.int32, gram.shape, 1)
    inverse = 1.0 / (jnp.sqrt(jnp.sum(jnp.where(row == col, gram, 0.0))) + norm_epsilon)
    store_upper(out_ref, composed(gram * inverse * inverse, ITERS) * inverse)


def shared_factor(own, part):
    return pl.pallas_call(
        factor_kernel,
        out_shape=jax.ShapeDtypeStruct((len(BLOCKS) * SIDE, SIDE), bf16),
        scratch_shapes=[pltpu.VMEM((COLS, COLS), f32)],
        compiler_params=pltpu.CompilerParams(vmem_limit_bytes=SMALL_GRANT),
        cost_estimate=pl.CostEstimate(flops=5 * 10**9, bytes_accessed=4 * own.size, transcendentals=0),
        name="factor",
    )(own, part)


def apply_kernel(which, in_ref, factor_ref, *refs):
    out_hbm, out_buf, full_ref, out_sem = refs[-4:]
    load_full(full_ref, factor_ref[...].astype(f32))
    peers, _, rows, cols = in_ref.shape
    step = peers // 4
    for k in range(4):
        part = pl.ds(k * step, step)
        product = times(in_ref[part, which].reshape(step * rows, cols), full_ref[...])
        out_buf[part] = product.reshape(step, rows, cols).astype(bf16)
        pltpu.make_async_copy(out_buf.at[part], out_hbm.at[part, which], out_sem).start()
    pltpu.make_async_copy(out_buf, out_hbm.at[:, which], out_sem).wait()


def applied(which, received, factor, before):
    earlier = () if before is None else (before,)
    vmem = pl.BlockSpec(memory_space=pltpu.VMEM)
    anywhere = pl.BlockSpec(memory_space=pl.ANY)
    return pl.pallas_call(
        functools.partial(apply_kernel, which),
        in_specs=[vmem, vmem] + [anywhere] * len(earlier),
        out_specs=anywhere,
        out_shape=jax.ShapeDtypeStruct(received.shape, bf16),
        scratch_shapes=[
            pltpu.VMEM(received.shape[:1] + received.shape[2:], bf16),
            pltpu.VMEM((COLS, COLS), bf16),
            pltpu.SemaphoreType.DMA(()),
        ],
        input_output_aliases={2: 0} if earlier else {},
        compiler_params=pltpu.CompilerParams(vmem_limit_bytes=SMALL_GRANT),
        cost_estimate=pl.CostEstimate(
            flops=received.size * COLS, bytes_accessed=3 * received.size, transcendentals=0
        ),
        name="apply",
    )(received, factor, *earlier)


def finish_kernel(pair_ref, ortho_ref, weight_ref, out_hbm, out_buf, sem):
    scale = learn_rate * 0.2 * math.sqrt(max(ROWS, COLS))
    pair = pair_ref[0]

    @pl.loop(0, ortho_ref.shape[0] // (2 * CHUNK))
    def _(chunk):
        base = chunk * (2 * CHUNK)
        for k in range(2 * CHUNK):
            matrix = base + rows_of(k // 2, 1 - k % 2, pair)
            kept = weight_ref[matrix].astype(f32) * (1.0 - learn_rate * weight_decay)
            out_buf[matrix] = (kept - scale * ortho_ref[base + k].astype(f32)).astype(bf16)
        rows = pl.ds(base, 2 * CHUNK)
        pltpu.make_async_copy(out_buf.at[rows], out_hbm.at[rows], sem).start()

    pltpu.make_async_copy(out_buf, out_hbm, sem).wait()


def finished(pair, ortho, weight):
    whole = pl.BlockSpec(weight.shape, lambda i, p: (0, 0, 0))
    return pl.pallas_call(
        finish_kernel,
        grid_spec=pltpu.PrefetchScalarGridSpec(
            num_scalar_prefetch=1,
            grid=(1,),
            in_specs=[whole, whole],
            out_specs=pl.BlockSpec(memory_space=pl.ANY),
            scratch_shapes=[pltpu.VMEM(weight.shape, bf16), pltpu.SemaphoreType.DMA(())],
        ),
        out_shape=jax.ShapeDtypeStruct(weight.shape, bf16),
        compiler_params=pltpu.CompilerParams(vmem_limit_bytes=24 << 20),
        cost_estimate=pl.CostEstimate(flops=3 * ortho.size, bytes_accessed=6 * ortho.size, transcendentals=0),
        name="finish",
    )(pair, ortho, weight)


def across(value):
    return lax.all_to_all(
        value, SPREAD, split_axis=0, concat_axis=0, axis_index_groups=exchange_groups(), tiled=True
    )


def opposite(value):
    moves = []
    for plane in range(4):
        for core in range(2):
            place = (plane - core) % 4
            moves.append((plane * 2 + core, (3 - place + core) % 4 * 2 + core))
    return lax.ppermute(value, (DEPTH, CORE), moves)


def local(weight, momentum, gradient, assign):
    grad = gradient[0]
    mom = momentum[0]
    slots = assign[0]
    plane = lax.axis_index(DEPTH) + lax.axis_size(DEPTH) - lax.axis_index(CORE)
    pair = (lax.rem(plane, 4) // 2).reshape(1)
    count = grad.size * lax.axis_size(ALL_AXES)
    partials, near_grad, near_mom = prepared(pair, slots, grad, mom)
    shared = lax.all_to_all(
        partials.reshape(DEVICES, 1, 128), ALL_AXES, split_axis=0, concat_axis=0, tiled=True
    ).reshape(DEVICES, 128)
    update = updated(count, shared, near_grad, near_mom)
    received = across(update)
    state = momentum_call(state_kernel, "state", count, slots, shared, grad, mom)
    received, state = lax.optimization_barrier((received, state))
    halves = received.reshape(-1, 2, *received.shape[1:])
    upper = jax.ShapeDtypeStruct((len(BLOCKS) * SIDE, SIDE), bf16)
    part = opposite(gram_call(far_kernel, "far", halves, upper))
    own = gram_call(own_kernel, "own", halves, jax.ShapeDtypeStruct((COLS, COLS), f32))
    factor = shared_factor(own, part)
    given = opposite(factor)
    result = applied(0, halves, given, applied(1, halves, factor, None))
    ortho = across(result.reshape(received.shape))
    return (finished(pair, ortho, weight[0])[None], state[None])


def solution(mesh):
    torus = Mesh(
        mesh.devices.reshape(4, 4, 4, 2, 2),
        ("rows_0", "rows_1", "rows_2", "experts_0", "experts_1"),
    )
    sharded = P(EXPERTS, None, ROWS_AXES, None)
    return jax.shard_map(
        local,
        mesh=torus,
        in_specs=(sharded, sharded, sharded, P(EXPERTS, None)),
        out_specs=(sharded, sharded),
        check_vma=False,
    )
```
